256 devices in a mesh: seq: 16 (over z_hi, x), head: 16 (over y, z_lo, core).
Axes of the slice: x: 4, y: 4, z: 8 (z_hi: 4, z_lo: 2; z = z_hi * 2 + z_lo), core: 2. Of those that a mesh axis runs over, the one named last changes fastest.
Arguments:
- inputs: bfloat16 [6144, 6144], P('seq', 'head'), may hold values from -6 to 6
- weights: bfloat16 [3, 6144, 4096], P(None, None, 'head'), may hold values from -0.078125 to 0.078125
- cotangent: bfloat16 [6144, 4096], P('seq', 'head'), may hold values from -0.29882812 to 0.29882812
- log_decay: float32 [6144, 32], P('seq', 'head'), may hold values from -1 to 0, as said below
Outputs:
- input_grad: bfloat16 [6144, 6144], P('seq', 'head')
The draws below stay inside these ranges and needn't reach their ends.
Inputs may be any that keep to these rules, and one draw needn't show every extreme that they name: `log_decay`: every entry is negative.
All inputs are finite; a program needn't handle non-finite values.
Results may differ from the reference program's by a relative error of at most 0.02.
Values may be sent and summed in bfloat16 or wider, within the bound.
No kernel may reach another device: no remote copies, remote signals or barrier semaphores. Data moves between devices by JAX's collectives and lax.ppermute only.
A program may use at most 64 MiB of HBM per device.

```python
import jax
import jax.numpy as jnp
from jax import lax

D = 6144
HD = 128
HEADS_DEV = 2
TOK_DEV = 384
HEAD_TOTAL = 32
TOKEN_POSITIONS = 6144
N_SEQ = 16
N_HEAD = 16


def draw_log_decay(key, part):
    key_collection = jax.random.split(key, 6)
    slow_share = 0.5
    slow_heads = jax.random.uniform(key_collection[0], (HEAD_TOTAL,)) < slow_share
    slow_rate = jnp.exp(jax.random.uniform(key_collection[1], (HEAD_TOTAL,), minval=jnp.log(0.1), maxval=0.0)) / TOKEN_POSITIONS
    fast_rate = jnp.exp(jax.random.uniform(key_collection[2], (HEAD_TOTAL,), minval=jnp.log(1.0 / 50.0), maxval=jnp.log(1.0 / 30.0)))
    baseline_rate = jnp.where(slow_heads, slow_rate, fast_rate)
    multiplier = jnp.exp(jax.random.uniform(key_collection[3], (TOKEN_POSITIONS, HEAD_TOTAL), minval=jnp.log(0.5), maxval=jnp.log(2.0)))
    spike_locations = jax.random.randint(key_collection[4], (3, HEAD_TOTAL), 0, TOKEN_POSITIONS)
    token_offsets = jnp.arange(TOKEN_POSITIONS)[:, None]
    spike_mask = jnp.zeros((TOKEN_POSITIONS, HEAD_TOTAL), jnp.int32)
    for index_value in range(3):
        spike_mask = spike_mask + (token_offsets == spike_locations[index_value][None, :]).astype(jnp.int32)
    spike_reduction = jnp.log(jax.random.uniform(key_collection[5], (TOKEN_POSITIONS, HEAD_TOTAL), minval=0.6, maxval=0.8))
    output_values = -baseline_rate[None, :] * multiplier + jnp.where(spike_mask > 0, spike_reduction, 0.0)
    return output_values.astype(jnp.float32)


def shard_levels(key, shape, cuts, smallest, top_value):
    loudness, own = 1.0, jax.random.fold_in(key, 6)
    for position, blocks in cuts:
        heights = jnp.exp(jax.random.uniform(jax.random.fold_in(own, position), (blocks,), jnp.float32, smallest / len(cuts), top_value / len(cuts)))
        loudness = loudness * jnp.repeat(heights, shape[position] // blocks).reshape([-1 if axis == position else 1 for axis in range(len(shape))])
    return loudness


def scatter_about(own_key, extent, width, most, cuts=(), dtype=jnp.bfloat16):
    drawn = width * jax.random.normal(own_key, extent, jnp.float32)
    if cuts:
        drawn = drawn * shard_levels(own_key, extent, cuts, -0.22, 0.18)
    return jnp.clip(drawn, -most, most).astype(dtype)


def setup_inputs(seed: int = 0) -> dict:
    streams_of = jax.random.split(jax.random.key(seed), 5)
    return {
        "inputs": scatter_about(streams_of[0], (TOKEN_POSITIONS, D), 1.0, 6.0, ((0, 16), (1, 16))),
        "weights": scatter_about(streams_of[1], (3, D, HEAD_TOTAL * HD), D ** -0.5, 0.078125, ((2, 16),)),
        "cotangent": scatter_about(streams_of[2], (TOKEN_POSITIONS, HEAD_TOTAL * HD), 0.04, 0.29882812, ((0, 16), (1, 16))),
        "log_decay": draw_log_decay(jax.random.fold_in(streams_of[4], 71), 0),
    }


def silu_slope(projected):
    sigma = jax.nn.sigmoid(projected)
    return sigma * (1.0 + projected * (1.0 - sigma))


def block_grads(queries, key_rows, value_rows, grad_out, running, state_in, grad_in):
    highest = lax.Precision.HIGHEST
    scale = queries.shape[2] ** -0.5
    shard_total = running[-1]
    token_offsets = jnp.arange(running.shape[0])
    causal = (token_offsets[:, None] >= token_offsets[None, :])[:, :, None]
    log_gap = running[:, None, :] - running[None, :, :]
    decay_matrix = jnp.where(causal, jnp.exp(jnp.where(causal, log_gap, 0.0)), 0.0)
    out_value = jnp.einsum("iha,jha->ijh", grad_out, value_rows, precision=highest) * decay_matrix
    query_key = jnp.einsum("iha,jha->ijh", queries, key_rows, precision=highest) * decay_matrix
    rise = jnp.exp(running)[:, :, None]
    fall = jnp.exp(shard_total[None, :] - running)[:, :, None]
    grad_query = scale * (jnp.einsum("ijh,jha->iha", out_value, key_rows, precision=highest)
                          + rise * jnp.einsum("ihb,hab->iha", grad_out, state_in, precision=highest))
    grad_key = scale * (jnp.einsum("ijh,iha->jha", out_value, queries, precision=highest)
                        + fall * jnp.einsum("jhb,hab->jha", value_rows, grad_in, precision=highest))
    grad_value = scale * (jnp.einsum("ijh,iha->jha", query_key, grad_out, precision=highest)
                          + fall * jnp.einsum("jha,hab->jhb", key_rows, grad_in, precision=highest))
    return grad_query, grad_key, grad_value


def shard_states(queries, key_rows, value_rows, grad_out, running):
    highest = lax.Precision.HIGHEST
    shard_total = running[-1]
    weighted_keys = key_rows * jnp.exp(shard_total[None, :] - running)[:, :, None]
    weighted_queries = queries * jnp.exp(running)[:, :, None]
    key_state = jnp.einsum("tha,thb->hab", weighted_keys, value_rows, precision=highest)
    query_state = jnp.einsum("tha,thb->hab", weighted_queries, grad_out, precision=highest)
    return key_state, query_state


def carry_step(state, item_pair):
    shard_total, local_state = item_pair
    return jnp.exp(shard_total)[:, None, None] * state + local_state, state


def reference(inputs, weights, cotangent, log_decay):
    head_count = log_decay.shape[1]
    head_size = weights.shape[2] // head_count
    shards = N_SEQ
    rows_each = TOK_DEV
    projected = jnp.stack([jnp.dot(inputs, weights[index_value], preferred_element_type=jnp.float32) for index_value in range(3)])
    queries = jax.nn.silu(projected[0]).astype(jnp.bfloat16)
    key_rows = jax.nn.silu(projected[1]).astype(jnp.bfloat16)
    value_rows = projected[2].astype(jnp.bfloat16)

    def split_heads(array):
        return array.astype(jnp.float32).reshape(shards, rows_each, head_count, head_size)

    query_blocks = split_heads(queries)
    key_blocks = split_heads(key_rows)
    value_blocks = split_heads(value_rows)
    grad_blocks = split_heads(cotangent)
    running = jnp.cumsum(log_decay.reshape(shards, rows_each, head_count), axis=1)
    totals = running[:, -1]
    key_state, query_state = jax.vmap(shard_states)(query_blocks, key_blocks, value_blocks, grad_blocks, running)
    zero_state = jnp.zeros((head_count, head_size, head_size), jnp.float32)
    _, state_in = lax.scan(carry_step, zero_state, (totals, key_state))
    _, grad_in = lax.scan(carry_step, zero_state, (totals, query_state), reverse=True)

    def apply_block(block_items):
        return block_grads(*block_items)

    grad_query, grad_key, grad_value = lax.map(apply_block, (query_blocks, key_blocks, value_blocks, grad_blocks, running, state_in, grad_in))
    columns = head_count * head_size
    grad_query = grad_query.reshape(-1, columns)
    grad_key = grad_key.reshape(-1, columns)
    grad_value = grad_value.reshape(-1, columns)
    grad_projected = jnp.stack([grad_query * silu_slope(projected[0]),
                                grad_key * silu_slope(projected[1]),
                                grad_value]).astype(jnp.bfloat16)
    group_cols = HEADS_DEV * head_size
    summed = jnp.zeros(inputs.shape, jnp.float32)
    for group in range(N_HEAD):
        first = group * group_cols
        partial_sum = jnp.zeros(inputs.shape, jnp.float32)
        for index_value in range(3):
            grad_piece = grad_projected[index_value][:, first:first + group_cols]
            weight_piece = weights[index_value][:, first:first + group_cols]
            partial_sum = partial_sum + jnp.dot(grad_piece, weight_piece.T, preferred_element_type=jnp.float32)
        rounded = lax.optimization_barrier(partial_sum.astype(jnp.bfloat16))
        summed = summed + rounded.astype(jnp.float32)
    return summed.astype(jnp.bfloat16)
```

```python
import functools

import jax
import jax.numpy as jnp
from jax import lax
from jax.experimental import pallas as pl
from jax.experimental.pallas import tpu as pltpu
from jax.sharding import PartitionSpec as P


F32 = jnp.float32
BF16 = jnp.bfloat16
ROWS = 384
HEAD = 128
HEADS = 2
COLS = HEADS * HEAD
BLOCK = 384
PAIR = 2 * BLOCK
N_Y, N_Z = 4, 2
N_X, N_ZHI = 4, 4
HDR = 16
VMEM = pl.BlockSpec(memory_space=pltpu.VMEM)
ANY = pl.BlockSpec(memory_space=pl.ANY)


def call(body, outs, ins, scratch=(), flops=0, moved=0, any_at=(), name=None, limit=24 << 20):
    specs = [ANY if i in any_at else VMEM for i in range(len(ins))]
    single = not isinstance(outs, (list, tuple))
    return pl.pallas_call(
        body,
        out_shape=outs,
        in_specs=specs,
        out_specs=VMEM if single else [VMEM] * len(outs),
        scratch_shapes=list(scratch),
        compiler_params=pltpu.CompilerParams(vmem_limit_bytes=limit),
        cost_estimate=pl.CostEstimate(flops=flops, bytes_accessed=moved, transcendentals=0),
        name=name,
    )(*ins)


def head_place():
    place = lax.axis_index("head")
    return place // 4, (place // 2) % 2, place % 2


def seq_place():
    place = lax.axis_index("seq")
    return place // 4, place % 4


def chip_index(dy, dz):
    y, z, _ = head_place()
    return lax.rem(y + dy + N_Y, N_Y) * N_Z + lax.rem(z + dz, N_Z)


def head_shift(value, dy=0, dz=0, core=0):
    pairs = []
    for i in range(16):
        y, z, c = i // 4, (i // 2) % 2, i % 2
        pairs.append((i, ((y + dy) % 4) * 4 + ((z + dz) % 2) * 2 + (c + core) % 2))
    return lax.ppermute(value, "head", pairs)


def seq_shift(value, dx=0, dz=0):
    pairs = [(i, ((i // 4 + dz) % 4) * 4 + (i % 4 + dx) % 4) for i in range(16)]
    return lax.ppermute(value, "seq", pairs)


def project(shifts, blocks, weights, total):
    n = len(shifts)
    first = total is None

    def body(*refs):
        refs = list(refs)
        pairs = [(refs.pop(0), refs.pop(0)) for _ in range(n)]
        w_ref = refs.pop(0)
        t_ref = None if first else refs.pop(0)
        o_ref, wbuf, xcat, sem = refs
        core = head_place()[2]
        copies = []
        for i, (dy, dz) in enumerate(shifts):
            start = pl.multiple_of(chip_index(dy, dz) * PAIR, PAIR)
            copy = pltpu.make_async_copy(
                w_ref.at[:, pl.ds(start, PAIR), :], wbuf.at[i], sem.at[i]
            )
            copy.start()
            copies.append(copy)
        for i, (own, other) in enumerate(pairs):
            xcat[i, :, pl.ds(pl.multiple_of(core * BLOCK, BLOCK), BLOCK)] = own[...]
            xcat[i, :, pl.ds(pl.multiple_of((1 - core) * BLOCK, BLOCK), BLOCK)] = other[...]
        for i in range(n):
            copies[i].wait()
            for m in range(3):
                cols = slice(m * COLS, (m + 1) * COLS)
                part = jnp.dot(xcat[i], wbuf[i, m], preferred_element_type=F32)
                if i == 0 and first:
                    o_ref[:, cols] = part
                elif i == 0:
                    o_ref[:, cols] = t_ref[:, cols] + part
                else:
                    o_ref[:, cols] += part

    ins = [b for pair in blocks for b in pair] + [weights] + ([] if first else [total])
    return call(
        body,
        jax.ShapeDtypeStruct((ROWS, 3 * COLS), F32),
        ins,
        [
            pltpu.VMEM((n, 3, PAIR, COLS), BF16),
            pltpu.VMEM((n, ROWS, PAIR), BF16),
            pltpu.SemaphoreType.DMA((n,)),
        ],
        flops=2 * n * ROWS * PAIR * 3 * COLS,
        moved=n * 3 * PAIR * COLS * 2,
        any_at=(2 * n,),
        name=f"project_{n}",
    )


def decay_matrix(running, running_row):
    def body(r_ref, rr_ref, o_ref):
        i = lax.broadcasted_iota(jnp.int32, (ROWS, ROWS), 0)
        j = lax.broadcasted_iota(jnp.int32, (ROWS, ROWS), 1)
        causal = i >= j
        for h in range(HEADS):
            gap = r_ref[:, h : h + 1] - rr_ref[h : h + 1, :]
            o_ref[h] = jnp.where(causal, jnp.exp(jnp.where(causal, gap, 0.0)), 0.0) * (
                HEAD**-0.5
            )

    return call(
        body,
        jax.ShapeDtypeStruct((HEADS, ROWS, ROWS), F32),
        [running, running_row],
        flops=10 * HEADS * ROWS * ROWS,
        moved=4 * HEADS * ROWS * ROWS,
        name="decays",
    )


def local_states(projected, cotangent, running):
    def body(p_ref, g_ref, r_ref, q_ref, k_ref, v_ref, m_ref):
        last = r_ref[ROWS - 1 : ROWS, :]
        for h in range(HEADS):
            cols = slice(h * HEAD, (h + 1) * HEAD)
            query = jax.nn.silu(p_ref[:, cols]).astype(BF16)
            key = jax.nn.silu(p_ref[:, COLS + h * HEAD : COLS + (h + 1) * HEAD]).astype(BF16)
            value = p_ref[:, 2 * COLS + h * HEAD : 2 * COLS + (h + 1) * HEAD].astype(BF16)
            q_ref[:, cols], k_ref[:, cols], v_ref[:, cols] = query, key, value
            run = r_ref[:, h : h + 1]
            fall = jnp.exp(last[:, h : h + 1] - run)
            rise = jnp.exp(run)
            tn = (((0,), (0,)), ((), ()))
            key_state = lax.dot_general(
                (key.astype(F32) * fall).astype(BF16), value, tn, preferred_element_type=F32
            )
            query_state = lax.dot_general(
                (query.astype(F32) * rise).astype(BF16),
                g_ref[:, cols],
                tn,
                preferred_element_type=F32,
            )
            m_ref[h * HEAD : (h + 1) * HEAD, :] = key_state.astype(BF16)
            m_ref[COLS + h * HEAD : COLS + (h + 1) * HEAD, :] = query_state.astype(BF16)
        header(m_ref, 2 * COLS, [last[:, h : h + 1] for h in range(HEADS)])

    act = jax.ShapeDtypeStruct((ROWS, COLS), BF16)
    return call(
        body,
        [act, act, act, jax.ShapeDtypeStruct((2 * COLS + HDR, HEAD), BF16)],
        [projected, cotangent, running],
        flops=8 * ROWS * HEAD * COLS,
        moved=ROWS * COLS * 16,
        name="states",
    )


def header(ref, row, totals):
    sub = lax.broadcasted_iota(jnp.int32, (HDR, HEAD), 0)
    block = jnp.zeros((HDR, HEAD), F32)
    for h in range(HEADS):
        total = jnp.broadcast_to(totals[h], (HDR, HEAD))
        high = total.astype(BF16).astype(F32)
        block = jnp.where(sub == h, high, block)
        block = jnp.where(sub == HEADS + h, total - high, block)
    ref[row : row + HDR, :] = block.astype(BF16)


def read_totals(ref, row):
    block = ref[row : row + HDR, :].astype(F32)
    return [block[h : h + 1, :] + block[HEADS + h : HEADS + h + 1, :] for h in range(HEADS)]


def inner_part(query, key, value, cotangent, decays):
    def body(q_ref, k_ref, v_ref, g_ref, d_ref, gq_ref, gk_ref, gv_ref):
        nt = (((1,), (1,)), ((), ()))
        tn = (((0,), (0,)), ((), ()))
        for h in range(HEADS):
            cols = slice(h * HEAD, (h + 1) * HEAD)
            q, k, v, g = q_ref[:, cols], k_ref[:, cols], v_ref[:, cols], g_ref[:, cols]
            decay = d_ref[h]
            out_value = (
                lax.dot_general(g, v, nt, preferred_element_type=F32) * decay
            ).astype(BF16)
            query_key = (
                lax.dot_general(q, k, nt, preferred_element_type=F32) * decay
            ).astype(BF16)
            gq_ref[:, cols] = jnp.dot(out_value, k, preferred_element_type=F32)
            gk_ref[:, cols] = lax.dot_general(out_value, q, tn, preferred_element_type=F32)
            gv_ref[:, cols] = lax.dot_general(query_key, g, tn, preferred_element_type=F32)

    part = jax.ShapeDtypeStruct((ROWS, COLS), F32)
    return call(
        body,
        [part] * 3,
        [query, key, value, cotangent, decays],
        flops=10 * ROWS * ROWS * COLS,
        moved=ROWS * COLS * 20,
        name="inner",
    )


def join_x(own, received):
    def body(own_ref, *refs):
        got = refs[:3]
        send = refs[3:6]
        keep_ref, scale_ref = refs[6:]
        z, x = seq_place()
        messages = [own_ref] + list(got)
        row = 2 * COLS
        totals = [read_totals(m, row) for m in messages]
        source = [lax.rem(x - s + N_X, N_X) for s in range(N_X)]
        for h in range(HEADS):
            zero = jnp.zeros((1, HEAD), F32)

            def between(low, high):
                out = zero
                for s in range(N_X):
                    inside = jnp.logical_and(source[s] > low, source[s] < high)
                    out = out + jnp.where(inside, totals[s][h], 0.0)
                return out

            key_all = jnp.zeros((HEAD, HEAD), F32)
            query_all = jnp.zeros((HEAD, HEAD), F32)
            key_before = jnp.zeros((HEAD, HEAD), F32)
            query_after = jnp.zeros((HEAD, HEAD), F32)
            for s in range(N_X):
                ks = messages[s][h * HEAD : (h + 1) * HEAD, :].astype(F32)
                qs = messages[s][COLS + h * HEAD : COLS + (h + 1) * HEAD, :].astype(F32)
                p = source[s]
                key_all += jnp.exp(between(p, N_X)) * ks
                query_all += jnp.exp(between(-1, p)) * qs
                if s:
                    key_before += jnp.where(p < x, jnp.exp(between(p, x)), 0.0) * ks
                    query_after += jnp.where(p > x, jnp.exp(between(x, p)), 0.0) * qs
            rows = slice(h * HEAD, (h + 1) * HEAD)
            keep_ref[rows, :] = key_before
            keep_ref[COLS + h * HEAD : COLS + (h + 1) * HEAD, :] = query_after
            scale_ref[h : h + 1, :] = jnp.exp(between(-1, x))
            scale_ref[HEADS + h : HEADS + h + 1, :] = jnp.exp(between(x, N_X))
            for s in range(1, N_ZHI):
                later = jnp.full((HEAD, HEAD), z + s) < N_ZHI
                send[s - 1][rows, :] = jnp.where(later, key_all, query_all).astype(BF16)
        group = [sum(totals[s][h] for s in range(N_X)) for h in range(HEADS)]
        for s in range(1, N_ZHI):
            header(send[s - 1], COLS, group)

    message = jax.ShapeDtypeStruct((COLS + HDR, HEAD), BF16)
    return call(
        body,
        [message] * 3
        + [jax.ShapeDtypeStruct((2 * COLS, HEAD), F32), jax.ShapeDtypeStruct((8, HEAD), F32)],
        [own] + list(received),
        flops=40 * COLS * HEAD,
        moved=COLS * HEAD * 20,
        name="join_x",
    )


def outer_part(received, keep, scale, projected, act, cotangent, inner, running):
    def body(*refs):
        got = refs[:3]
        keep_ref, scale_ref, p_ref, q_ref, k_ref, v_ref, g_ref = refs[3:10]
        gq_ref, gk_ref, gv_ref, r_ref, o_ref = refs[10:]
        z, _ = seq_place()
        nt = (((1,), (1,)), ((), ()))
        source = [lax.rem(z - s + N_ZHI, N_ZHI) for s in range(1, N_ZHI)]
        totals = [read_totals(m, COLS) for m in got]
        c = HEAD**-0.5
        last = r_ref[ROWS - 1 : ROWS, :]

        def slope(v):
            s = jax.nn.sigmoid(v)
            return s * (1.0 + v * (1.0 - s))

        for h in range(HEADS):
            cols = slice(h * HEAD, (h + 1) * HEAD)

            def between(low, high):
                out = jnp.zeros((1, HEAD), F32)
                for s in range(N_ZHI - 1):
                    inside = jnp.logical_and(source[s] > low, source[s] < high)
                    out = out + jnp.where(inside, totals[s][h], 0.0)
                return out

            before = jnp.zeros((HEAD, HEAD), F32)
            after = jnp.zeros((HEAD, HEAD), F32)
            for s in range(N_ZHI - 1):
                p = source[s]
                state = got[s][cols, :].astype(F32)
                before += jnp.where(p < z, jnp.exp(between(p, z)), 0.0) * state
                after += jnp.where(p > z, jnp.exp(between(z, p)), 0.0) * state
            state_in = (keep_ref[cols, :] + scale_ref[h : h + 1, :] * before).astype(BF16)
            grad_in = (
                keep_ref[COLS + h * HEAD : COLS + (h + 1) * HEAD, :]
                + scale_ref[HEADS + h : HEADS + h + 1, :] * after
            ).astype(BF16)
            run = r_ref[:, h : h + 1]
            rise = jnp.exp(run) * c
            fall = jnp.exp(last[:, h : h + 1] - run) * c
            grad_query = gq_ref[:, cols] + rise * lax.dot_general(
                g_ref[:, cols], state_in, nt, preferred_element_type=F32
            )
            grad_key = gk_ref[:, cols] + fall * lax.dot_general(
                v_ref[:, cols], grad_in, nt, preferred_element_type=F32
            )
            grad_value = gv_ref[:, cols] + fall * jnp.dot(
                k_ref[:, cols], grad_in, preferred_element_type=F32
            )
            grads = (
                grad_query * slope(p_ref[:, cols]),
                grad_key * slope(p_ref[:, COLS + h * HEAD : COLS + (h + 1) * HEAD]),
                grad_value,
            )
            for m in range(3):
                at = m * COLS + h * HEAD
                o_ref[at : at + HEAD, :] = grads[m].T.astype(BF16)

    return call(
        body,
        jax.ShapeDtypeStruct((3 * COLS, ROWS), BF16),
        list(received) + [keep, scale, projected] + list(act) + [cotangent] + list(inner) + [running],
        flops=6 * ROWS * HEAD * COLS,
        moved=ROWS * COLS * 40,
        name="outer",
    )


def partials(shifts, grads, weights, received, own_core):
    n = len(shifts)
    add = received is not None

    def body(*refs):
        refs = list(refs)
        g_ref, w_ref = refs.pop(0), refs.pop(0)
        r_ref = refs.pop(0) if add else None
        outs, (wbuf, sem) = refs[:-2], refs[-2:]
        core = head_place()[2]
        if not own_core:
            core = 1 - core
        copies = []
        for i, (dy, dz) in enumerate(shifts):
            start = pl.multiple_of((chip_index(dy, dz) * 2 + core) * BLOCK, BLOCK)
            copy = pltpu.make_async_copy(
                w_ref.at[:, pl.ds(start, BLOCK), :], wbuf.at[i], sem.at[i]
            )
            copy.start()
            copies.append(copy)
        for i in range(n):
            copies[i].wait()
            part = None
            for m in range(3):
                term = jnp.dot(
                    wbuf[i, m], g_ref[m * COLS : (m + 1) * COLS, :], preferred_element_type=F32
                )
                part = term if part is None else part + term
            if add:
                outs[i][...] = (part + r_ref[i].astype(F32)).astype(BF16)
            else:
                outs[0][i] = part.astype(BF16)

    block = jax.ShapeDtypeStruct((BLOCK, ROWS), BF16)
    return call(
        body,
        [block] * n if add else [jax.ShapeDtypeStruct((n, BLOCK, ROWS), BF16)],
        [grads, weights] + ([received] if add else []),
        [pltpu.VMEM((n, 3, BLOCK, COLS), BF16), pltpu.SemaphoreType.DMA((n,))],
        flops=2 * n * ROWS * BLOCK * 3 * COLS,
        moved=n * 3 * BLOCK * COLS * 2,
        any_at=(1,),
        name=f"partial_{n}_{int(add)}",
    )


def add_pair(a, b):
    def body(a_ref, b_ref, o_ref):
        o_ref[...] = (a_ref[...].astype(F32) + b_ref[...].astype(F32)).astype(BF16)

    return call(
        body,
        jax.ShapeDtypeStruct((BLOCK, ROWS), BF16),
        [a, b],
        flops=BLOCK * ROWS,
        moved=BLOCK * ROWS * 6,
        name="add_pair",
    )


def finish(parts):
    def body(*refs):
        total = refs[0][...].astype(F32)
        for ref in refs[1:-1]:
            total = total + ref[...].astype(F32)
        refs[-1][...] = total.T.astype(BF16)

    return call(
        body,
        jax.ShapeDtypeStruct((ROWS, BLOCK), BF16),
        list(parts),
        flops=5 * BLOCK * ROWS,
        moved=BLOCK * ROWS * 12,
        name="finish",
    )


def on_device(inputs, weights, cotangent, log_decay):
    running = jnp.cumsum(log_decay, axis=0)
    decays = decay_matrix(running, running.T)

    far = head_shift(inputs, dy=2)
    side = head_shift(inputs, dz=1)
    up = head_shift(inputs, dy=1)
    down = head_shift(inputs, dy=-1)
    own_other = head_shift(inputs, core=1)
    total = project([(0, 0)], [(inputs, own_other)], weights, None)
    far_side = head_shift(side, dy=2)
    up_side = head_shift(up, dz=1)
    down_side = head_shift(down, dz=1)
    first = head_shift(jnp.stack([side, up, down, far]), core=1)
    total = project(
        [(0, 1), (-1, 0), (1, 0), (2, 0)],
        [(side, first[0]), (up, first[1]), (down, first[2]), (far, first[3])],
        weights,
        total,
    )
    second = head_shift(jnp.stack([far_side, up_side, down_side]), core=1)
    total = project(
        [(2, 1), (-1, 1), (1, 1)],
        [(far_side, second[0]), (up_side, second[1]), (down_side, second[2])],
        weights,
        total,
    )

    query, key, value, message = local_states(total, cotangent, running)
    over_x = [seq_shift(message, dx=s) for s in (1, 2, 3)]
    inner = inner_part(query, key, value, cotangent, decays)
    *send, keep, scale = join_x(message, over_x)
    over_z = [seq_shift(send[s - 1], dz=s) for s in (1, 2, 3)]
    grads = outer_part(
        over_z, keep, scale, total, (query, key, value), cotangent, inner, running
    )

    ring_a = [(1, 1), (-1, 1), (2, 1), (2, 0)]
    ring_b = [(1, 0), (-1, 0), (0, 1), (0, 0)]
    (other_a,) = partials(ring_a, grads, weights, None, False)
    got_a = head_shift(other_a, core=1)
    (other_b,) = partials(ring_b, grads, weights, None, False)
    got_b = head_shift(other_b, core=1)
    up_side, down_side, far_side, far = partials(ring_a, grads, weights, got_a, True)
    r_up = head_shift(up_side, dz=1)
    r_down = head_shift(down_side, dz=1)
    r_side = head_shift(far_side, dy=2)
    r_far = head_shift(far, dy=2)
    up, down, side, mine = partials(ring_b, grads, weights, got_b, True)
    r_up = head_shift(add_pair(up, r_up), dy=1)
    r_side = head_shift(add_pair(side, r_side), dz=1)
    r_down = head_shift(add_pair(down, r_down), dy=-1)
    return finish([mine, r_far, r_up, r_down, r_side])


def solution(mesh):
    placed = (P("seq", "head"), P(None, None, "head"), P("seq", "head"), P("seq", "head"))
    return jax.shard_map(
        on_device, mesh=mesh, in_specs=placed, out_specs=P("seq", "head"), check_vma=False
    )
```

```python
import jax
import jax.numpy as jnp
from jax import lax
from jax.experimental import pallas as pl
from jax.experimental.pallas import tpu as pltpu
from jax.sharding import PartitionSpec as P


SEQ_AXIS, HEAD_AXIS = "seq", "head"
F32 = jnp.float32
BF16 = jnp.bfloat16
ROWS = 384
HEAD = 128
HEADS = 2
COLS = HEADS * HEAD
BLOCK = 384
PAIR = 2 * BLOCK
N_Y, N_Z = 4, 2
N_X, N_ZHI = 4, 4
HDR = 16
VMEM = pl.BlockSpec(memory_space=pltpu.VMEM)
HBM = pl.BlockSpec(memory_space=pltpu.HBM)


def call(body, outs, ins, scratch=(), flops=0, moved=0, hbm_at=(), limit=8 << 20):
    specs = [HBM if i in hbm_at else VMEM for i in range(len(ins))]
    single = not isinstance(outs, (list, tuple))
    return pl.pallas_call(
        body,
        out_shape=outs,
        in_specs=specs,
        out_specs=VMEM if single else [VMEM] * len(outs),
        scratch_shapes=list(scratch),
        compiler_params=pltpu.CompilerParams(vmem_limit_bytes=limit),
        cost_estimate=pl.CostEstimate(flops=flops, bytes_accessed=moved, transcendentals=0),
    )(*ins)


def head_place():
    place = lax.axis_index(HEAD_AXIS)
    return place // 4, (place // 2) % 2, place % 2


def seq_place():
    place = lax.axis_index(SEQ_AXIS)
    return place // 4, place % 4


def chip_index(shift, core):
    dy, times, dz = shift
    y, z, _ = head_place()
    step = y + (dy + N_Y)
    if times:
        step = step + times * (2 * core - 1)
    return lax.rem(step, N_Y) * N_Z + lax.rem(z + dz, N_Z)


def head_shift(value, dy=0, dz=0, core=0):
    pairs = []
    for i in range(16):
        y, z, c = i // 4, (i // 2) % 2, i % 2
        pairs.append((i, ((y + dy) % 4) * 4 + ((z + dz) % 2) * 2 + (c + core) % 2))
    return lax.ppermute(value, HEAD_AXIS, pairs)


def head_turn(value, dy):
    pairs = []
    for i in range(16):
        y, rest = i // 4, i % 4
        step = -dy if i % 2 else dy
        pairs.append((i, ((y + step) % 4) * 4 + rest))
    return lax.ppermute(value, HEAD_AXIS, pairs)


def seq_shift(value, dx=0, dz=0):
    pairs = [(i, ((i // 4 + dz) % 4) * 4 + (i % 4 + dx) % 4) for i in range(16)]
    return lax.ppermute(value, SEQ_AXIS, pairs)


def load(weights, cotangent):
    def body(w_ref, g_ref, o_ref, og_ref, sem):
        copies = [pltpu.make_async_copy(g_ref, og_ref, sem.at[3])]
        copies += [pltpu.make_async_copy(w_ref.at[m], o_ref.at[m], sem.at[m]) for m in range(3)]
        for copy in copies:
            copy.start()
        for copy in copies:
            copy.wait()

    return call(
        body,
        [pltpu.VMEM(weights.shape, BF16), pltpu.VMEM(cotangent.shape, BF16)],
        [pltpu.with_memory_space_constraint(x, pltpu.HBM) for x in (weights, cotangent)],
        [pltpu.SemaphoreType.DMA((4,))],
        moved=2 * weights.size,
        hbm_at=(0, 1),
        limit=4 << 20,
    )


def project(shifts, blocks, weights, total):
    n = len(shifts)
    first = total is None

    def body(*refs):
        refs = list(refs)
        pairs = [(refs.pop(0), refs.pop(0)) for _ in range(n)]
        w_ref = refs.pop(0)
        t_ref = None if first else refs.pop(0)
        o_ref, xcat = refs
        core = head_place()[2]
        for i, (own, other) in enumerate(pairs):
            xcat[i, :, pl.ds(pl.multiple_of(core * BLOCK, BLOCK), BLOCK)] = own[...]
            xcat[i, :, pl.ds(pl.multiple_of((1 - core) * BLOCK, BLOCK), BLOCK)] = other[...]
        for i, shift in enumerate(shifts):
            rows = pl.ds(pl.multiple_of(chip_index(shift, core) * PAIR, PAIR), PAIR)
            for m in range(3):
                cols = slice(m * COLS, (m + 1) * COLS)
                part = jnp.dot(xcat[i], w_ref[m, rows, :], preferred_element_type=F32)
                if i == 0 and first:
                    o_ref[:, cols] = part
                elif i == 0:
                    o_ref[:, cols] = t_ref[:, cols] + part
                else:
                    o_ref[:, cols] += part

    return call(
        body,
        jax.ShapeDtypeStruct((ROWS, 3 * COLS), F32),
        [b for pair in blocks for b in pair] + [weights] + ([] if first else [total]),
        [pltpu.VMEM((n, ROWS, PAIR), BF16)],
        flops=2 * n * ROWS * PAIR * 3 * COLS,
        moved=n * 3 * PAIR * COLS * 2,
    )


def project_half(shift, block, weights, total, own_core):
    def body(x_ref, w_ref, t_ref, o_ref):
        core = head_place()[2]
        if not own_core:
            core = 1 - core
        rows = pl.ds(pl.multiple_of((chip_index(shift, core) * 2 + core) * BLOCK, BLOCK), BLOCK)
        for m in range(3):
            cols = slice(m * COLS, (m + 1) * COLS)
            o_ref[:, cols] = t_ref[:, cols] + jnp.dot(
                x_ref[...], w_ref[m, rows, :], preferred_element_type=F32
            )

    return call(
        body,
        jax.ShapeDtypeStruct((ROWS, 3 * COLS), F32),
        [block, weights, total],
        flops=2 * ROWS * BLOCK * 3 * COLS,
        moved=3 * BLOCK * COLS * 2,
    )


def decay_matrix(log_decay_row):
    def body(l_ref, o_ref, r_ref):
        i = lax.broadcasted_iota(jnp.int32, (ROWS, ROWS), 0)
        j = lax.broadcasted_iota(jnp.int32, (ROWS, ROWS), 1)
        causal = i >= j
        lower = causal.astype(F32)
        logs = jnp.concatenate([l_ref[...], jnp.zeros((8 - HEADS, ROWS), F32)], axis=0)
        nt = (((1,), (1,)), ((), ()))
        highest = lax.Precision.HIGHEST
        column = lax.dot_general(lower, logs, nt, precision=highest, preferred_element_type=F32)
        row = lax.dot_general(logs, lower, nt, precision=highest, preferred_element_type=F32)
        r_ref[...] = column[:, :HEADS]
        for h in range(HEADS):
            gap = column[:, h : h + 1] - row[h : h + 1, :]
            o_ref[h] = jnp.where(causal, jnp.exp(jnp.where(causal, gap, 0.0)), 0.0) * (
                HEAD**-0.5
            )

    return call(
        body,
        [
            jax.ShapeDtypeStruct((HEADS, ROWS, ROWS), F32),
            jax.ShapeDtypeStruct((ROWS, HEADS), F32),
        ],
        [log_decay_row],
        flops=10 * HEADS * ROWS * ROWS,
        moved=4 * HEADS * ROWS * ROWS,
    )


def local_states(projected, cotangent, running):
    def body(p_ref, g_ref, r_ref, q_ref, k_ref, v_ref, m_ref):
        last = r_ref[ROWS - 1 : ROWS, :]
        for h in range(HEADS):
            cols = slice(h * HEAD, (h + 1) * HEAD)
            query = jax.nn.silu(p_ref[:, cols]).astype(BF16)
            key = jax.nn.silu(p_ref[:, COLS + h * HEAD : COLS + (h + 1) * HEAD]).astype(BF16)
            value = p_ref[:, 2 * COLS + h * HEAD : 2 * COLS + (h + 1) * HEAD].astype(BF16)
            q_ref[:, cols], k_ref[:, cols], v_ref[:, cols] = query, key, value
            run = r_ref[:, h : h + 1]
            fall = jnp.exp(last[:, h : h + 1] - run)
            rise = jnp.exp(run)
            tn = (((0,), (0,)), ((), ()))
            key_state = lax.dot_general(
                (key.astype(F32) * fall).astype(BF16), value, tn, preferred_element_type=F32
            )
            query_state = lax.dot_general(
                (query.astype(F32) * rise).astype(BF16),
                g_ref[:, cols],
                tn,
                preferred_element_type=F32,
            )
            m_ref[h * HEAD : (h + 1) * HEAD, :] = key_state.astype(BF16)
            m_ref[COLS + h * HEAD : COLS + (h + 1) * HEAD, :] = query_state.astype(BF16)
        header(m_ref, 2 * COLS, [last[:, h : h + 1] for h in range(HEADS)])

    act = jax.ShapeDtypeStruct((ROWS, COLS), BF16)
    return call(
        body,
        [act, act, act, jax.ShapeDtypeStruct((2 * COLS + HDR, HEAD), BF16)],
        [projected, cotangent, running],
        flops=8 * ROWS * HEAD * COLS,
        moved=ROWS * COLS * 16,
    )


def header(ref, row, totals):
    sub = lax.broadcasted_iota(jnp.int32, (HDR, HEAD), 0)
    block = jnp.zeros((HDR, HEAD), F32)
    for h in range(HEADS):
        total = jnp.broadcast_to(totals[h], (HDR, HEAD))
        high = total.astype(BF16).astype(F32)
        block = jnp.where(sub == h, high, block)
        block = jnp.where(sub == HEADS + h, total - high, block)
    ref[row : row + HDR, :] = block.astype(BF16)


def read_totals(ref, row):
    block = ref[row : row + HDR, :].astype(F32)
    return [block[h : h + 1, :] + block[HEADS + h : HEADS + h + 1, :] for h in range(HEADS)]


def inner_part(query, key, value, cotangent, decays):
    def body(q_ref, k_ref, v_ref, g_ref, d_ref, gq_ref, gk_ref, gv_ref):
        nt = (((1,), (1,)), ((), ()))
        tn = (((0,), (0,)), ((), ()))
        for h in range(HEADS):
            cols = slice(h * HEAD, (h + 1) * HEAD)
            q, k, v, g = q_ref[:, cols], k_ref[:, cols], v_ref[:, cols], g_ref[:, cols]
            decay = d_ref[h]
            out_value = (
                lax.dot_general(g, v, nt, preferred_element_type=F32) * decay
            ).astype(BF16)
            query_key = (
                lax.dot_general(q, k, nt, preferred_element_type=F32) * decay
            ).astype(BF16)
            gq_ref[:, cols] = jnp.dot(out_value, k, preferred_element_type=F32)
            gk_ref[:, cols] = lax.dot_general(out_value, q, tn, preferred_element_type=F32)
            gv_ref[:, cols] = lax.dot_general(query_key, g, tn, preferred_element_type=F32)

    part = jax.ShapeDtypeStruct((ROWS, COLS), F32)
    return call(
        body,
        [part] * 3,
        [query, key, value, cotangent, decays],
        flops=10 * ROWS * ROWS * COLS,
        moved=ROWS * COLS * 20,
    )


def join_x(own, received):
    def body(own_ref, *refs):
        got = refs[:3]
        send = refs[3:6]
        keep_ref, scale_ref = refs[6:]
        z, x = seq_place()
        messages = [own_ref] + list(got)
        row = 2 * COLS
        totals = [read_totals(m, row) for m in messages]
        source = [lax.rem(x - s + N_X, N_X) for s in range(N_X)]
        for h in range(HEADS):
            zero = jnp.zeros((1, HEAD), F32)

            def between(low, high):
                out = zero
                for s in range(N_X):
                    inside = jnp.logical_and(source[s] > low, source[s] < high)
                    out = out + jnp.where(inside, totals[s][h], 0.0)
                return out

            key_all = jnp.zeros((HEAD, HEAD), F32)
            query_all = jnp.zeros((HEAD, HEAD), F32)
            key_before = jnp.zeros((HEAD, HEAD), F32)
            query_after = jnp.zeros((HEAD, HEAD), F32)
            for s in range(N_X):
                ks = messages[s][h * HEAD : (h + 1) * HEAD, :].astype(F32)
                qs = messages[s][COLS + h * HEAD : COLS + (h + 1) * HEAD, :].astype(F32)
                p = source[s]
                key_all += jnp.exp(between(p, N_X)) * ks
                query_all += jnp.exp(between(-1, p)) * qs
                if s:
                    key_before += jnp.where(p < x, jnp.exp(between(p, x)), 0.0) * ks
                    query_after += jnp.where(p > x, jnp.exp(between(x, p)), 0.0) * qs
            rows = slice(h * HEAD, (h + 1) * HEAD)
            keep_ref[rows, :] = key_before
            keep_ref[COLS + h * HEAD : COLS + (h + 1) * HEAD, :] = query_after
            scale_ref[h : h + 1, :] = jnp.exp(between(-1, x))
            scale_ref[HEADS + h : HEADS + h + 1, :] = jnp.exp(between(x, N_X))
            for s in range(1, N_ZHI):
                later = jnp.full((HEAD, HEAD), z + s) < N_ZHI
                send[s - 1][rows, :] = jnp.where(later, key_all, query_all).astype(BF16)
        group = [sum(totals[s][h] for s in range(N_X)) for h in range(HEADS)]
        for s in range(1, N_ZHI):
            header(send[s - 1], COLS, group)

    message = jax.ShapeDtypeStruct((COLS + HDR, HEAD), BF16)
    return call(
        body,
        [message] * 3
        + [jax.ShapeDtypeStruct((2 * COLS, HEAD), F32), jax.ShapeDtypeStruct((8, HEAD), F32)],
        [own] + list(received),
        flops=40 * COLS * HEAD,
        moved=COLS * HEAD * 20,
    )


def outer_part(received, keep, scale, projected, act, cotangent, inner, running):
    def body(*refs):
        got = refs[:3]
        keep_ref, scale_ref, p_ref, _, k_ref, v_ref, g_ref = refs[3:10]
        gq_ref, gk_ref, gv_ref, r_ref, o_ref = refs[10:]
        z, _ = seq_place()
        nt = (((1,), (1,)), ((), ()))
        source = [lax.rem(z - s + N_ZHI, N_ZHI) for s in range(1, N_ZHI)]
        totals = [read_totals(m, COLS) for m in got]
        c = HEAD**-0.5
        last = r_ref[ROWS - 1 : ROWS, :]

        def slope(v):
            s = jax.nn.sigmoid(v)
            return s * (1.0 + v * (1.0 - s))

        for h in range(HEADS):
            cols = slice(h * HEAD, (h + 1) * HEAD)

            def between(low, high):
                out = jnp.zeros((1, HEAD), F32)
                for s in range(N_ZHI - 1):
                    inside = jnp.logical_and(source[s] > low, source[s] < high)
                    out = out + jnp.where(inside, totals[s][h], 0.0)
                return out

            before = jnp.zeros((HEAD, HEAD), F32)
            after = jnp.zeros((HEAD, HEAD), F32)
            for s in range(N_ZHI - 1):
                p = source[s]
                state = got[s][cols, :].astype(F32)
                before += jnp.where(p < z, jnp.exp(between(p, z)), 0.0) * state
                after += jnp.where(p > z, jnp.exp(between(z, p)), 0.0) * state
            state_in = (keep_ref[cols, :] + scale_ref[h : h + 1, :] * before).astype(BF16)
            grad_in = (
                keep_ref[COLS + h * HEAD : COLS + (h + 1) * HEAD, :]
                + scale_ref[HEADS + h : HEADS + h + 1, :] * after
            ).astype(BF16)
            run = r_ref[:, h : h + 1]
            rise = jnp.exp(run) * c
            fall = jnp.exp(last[:, h : h + 1] - run) * c
            grad_query = gq_ref[:, cols] + rise * lax.dot_general(
                g_ref[:, cols], state_in, nt, preferred_element_type=F32
            )
            grad_key = gk_ref[:, cols] + fall * lax.dot_general(
                v_ref[:, cols], grad_in, nt, preferred_element_type=F32
            )
            grad_value = gv_ref[:, cols] + fall * jnp.dot(
                k_ref[:, cols], grad_in, preferred_element_type=F32
            )
            grads = (
                grad_query * slope(p_ref[:, cols]),
                grad_key * slope(p_ref[:, COLS + h * HEAD : COLS + (h + 1) * HEAD]),
                grad_value,
            )
            for m in range(3):
                at = m * COLS + h * HEAD
                o_ref[at : at + HEAD, :] = grads[m].T.astype(BF16)

    return call(
        body,
        jax.ShapeDtypeStruct((3 * COLS, ROWS), BF16),
        list(received) + [keep, scale, projected] + list(act) + [cotangent] + list(inner) + [running],
        flops=6 * ROWS * HEAD * COLS,
        moved=ROWS * COLS * 40,
    )


def partials(shifts, grads, weights, received, own_core, dtype=BF16):
    n = len(shifts)
    add = received is not None

    def body(*refs):
        refs = list(refs)
        g_ref, w_ref = refs.pop(0), refs.pop(0)
        r_ref = refs.pop(0) if add else None
        outs = refs
        core = head_place()[2]
        if not own_core:
            core = 1 - core
        for i, shift in enumerate(shifts):
            block = chip_index(shift, core) * 2 + core
            rows = pl.ds(pl.multiple_of(block * BLOCK, BLOCK), BLOCK)
            part = None
            for m in range(3):
                term = jnp.dot(
                    w_ref[m, rows, :],
                    g_ref[m * COLS : (m + 1) * COLS, :],
                    preferred_element_type=F32,
                )
                part = term if part is None else part + term
            if add:
                outs[i][...] = (part + r_ref[i].astype(F32)).astype(BF16)
            else:
                outs[0][i] = part.astype(dtype)

    block = jax.ShapeDtypeStruct((BLOCK, ROWS), BF16)
    return call(
        body,
        [block] * n if add else [jax.ShapeDtypeStruct((n, BLOCK, ROWS), dtype)],
        [grads, weights] + ([received] if add else []),
        flops=2 * n * ROWS * BLOCK * 3 * COLS,
        moved=n * 3 * BLOCK * COLS * 2,
    )


def add_cores(own, received):
    def body(a_ref, b_ref, *outs):
        for i, out in enumerate(outs):
            out[...] = (a_ref[i] + b_ref[i].astype(F32)).astype(BF16)

    n = own.shape[0]
    return call(
        body,
        [jax.ShapeDtypeStruct((BLOCK, ROWS), BF16)] * n,
        [own, received],
        flops=n * BLOCK * ROWS,
        moved=n * BLOCK * ROWS * 8,
    )


def add_all(parts):
    def body(*refs):
        total = refs[0][...].astype(F32)
        for ref in refs[1:-1]:
            total = total + ref[...].astype(F32)
        refs[-1][...] = total.astype(BF16)

    return call(
        body,
        jax.ShapeDtypeStruct((BLOCK, ROWS), BF16),
        list(parts),
        flops=len(parts) * BLOCK * ROWS,
        moved=BLOCK * ROWS * 2 * (len(parts) + 1),
    )


def finish(parts):
    def body(*refs):
        total = refs[0][...].astype(F32)
        for ref in refs[1:-1]:
            total = total + ref[...].astype(F32)
        refs[-1][...] = total.T.astype(BF16)

    return call(
        body,
        jax.ShapeDtypeStruct((ROWS, BLOCK), BF16),
        list(parts),
        flops=5 * BLOCK * ROWS,
        moved=BLOCK * ROWS * 12,
    )


OWN, FAR, TURN, BACK = (0, 0, 0), (2, 0, 0), (0, 1, 0), (0, -1, 0)
SIDE, FAR_SIDE, TURN_SIDE, BACK_SIDE = (0, 0, 1), (2, 0, 1), (0, 1, 1), (0, -1, 1)
GROUPS = (
    ((FAR_SIDE,), True),
    ((TURN_SIDE,), True),
    ((BACK_SIDE, FAR), True),
    ((SIDE, BACK), False),
    ((TURN, OWN), False),
)


def layer(inputs, weights, cotangent, log_decay):
    decays, running = decay_matrix(log_decay.T)

    turn = head_turn(inputs, 1)
    back = head_turn(inputs, -1)
    side = head_shift(inputs, dz=1)
    turn_side = head_shift(turn, dz=1)
    far = head_turn(turn, 1)
    back_side = head_turn(side, -1)
    far_side = head_turn(turn_side, 1)

    def other(block):
        return head_shift(block, core=1)

    resident, cotangent = load(weights, cotangent)
    total = project([OWN], [(inputs, other(inputs))], resident, None)
    total = project([TURN, BACK], [(turn, other(back)), (back, other(turn))], resident, total)
    total = project([SIDE], [(side, other(side))], resident, total)
    total = project([FAR], [(far, other(far))], resident, total)
    total = project(
        [TURN_SIDE, BACK_SIDE],
        [(turn_side, other(back_side)), (back_side, other(turn_side))],
        resident,
        total,
    )
    far_other = other(far_side)
    total = project_half(FAR_SIDE, far_side, resident, total, True)
    total = project_half(FAR_SIDE, far_other, resident, total, False)

    query, key, value, message = local_states(total, cotangent, running)
    over_x = [seq_shift(message, dx=s) for s in (1, 2, 3)]
    inner = inner_part(query, key, value, cotangent, decays)
    *send, keep, scale = join_x(message, over_x)
    over_z = [seq_shift(send[s - 1], dz=s) for s in (1, 2, 3)]
    grads = outer_part(
        over_z, keep, scale, total, (query, key, value), cotangent, inner, running
    )

    blocks = {}
    for group, apart in GROUPS:
        (share,) = partials(group, grads, resident, None, False)
        got = head_shift(share, core=1)
        if apart:
            (own,) = partials(group, grads, resident, None, True, F32)
            done = add_cores(own, got)
        else:
            done = partials(group, grads, resident, got, True)
        blocks.update(zip(group, done))
    far_side = head_turn(blocks[FAR_SIDE], -1)
    back_side = head_turn(blocks[BACK_SIDE], 1)
    far = head_turn(blocks[FAR], -1)
    back = head_turn(blocks[BACK], 1)
    turn_side = head_shift(add_all([blocks[TURN_SIDE], far_side]), dz=1)
    side = head_shift(add_all([blocks[SIDE], back_side]), dz=1)
    turn = head_turn(add_all([blocks[TURN], far, turn_side]), -1)
    return finish([blocks[OWN], back, side, turn])


def solution(mesh):
    rows = P(SEQ_AXIS, HEAD_AXIS)
    return jax.shard_map(
        layer,
        mesh=mesh,
        in_specs=(rows, P(None, None, HEAD_AXIS), rows, rows),
        out_specs=rows,
        check_vma=False,
    )
```

```python
import jax
import jax.numpy as jnp
from jax import lax
from jax.experimental import pallas as pl
from jax.experimental.pallas import tpu as pltpu
from jax.sharding import PartitionSpec as P


SEQ_AXIS, HEAD_AXIS = "seq", "head"
F32 = jnp.float32
BF16 = jnp.bfloat16
ROWS = 384
HEAD = 128
HEADS = 2
COLS = HEADS * HEAD
BLOCK = 384
PAIR = 2 * BLOCK
N_Y, N_Z = 4, 2
N_X, N_ZHI = 4, 4
HDR = 16
VMEM = pl.BlockSpec(memory_space=pltpu.VMEM)
HBM = pl.BlockSpec(memory_space=pltpu.HBM)


def call(body, outs, ins, scratch=(), flops=0, moved=0, hbm_at=(), limit=8 << 20):
    specs = [HBM if i in hbm_at else VMEM for i in range(len(ins))]
    single = not isinstance(outs, (list, tuple))
    return pl.pallas_call(
        body,
        out_shape=outs,
        in_specs=specs,
        out_specs=VMEM if single else [VMEM] * len(outs),
        scratch_shapes=list(scratch),
        compiler_params=pltpu.CompilerParams(vmem_limit_bytes=limit),
        cost_estimate=pl.CostEstimate(flops=flops, bytes_accessed=moved, transcendentals=0),
    )(*ins)


def head_place():
    place = lax.axis_index(HEAD_AXIS)
    return place // 4, (place // 2) % 2, place % 2


def seq_place():
    place = lax.axis_index(SEQ_AXIS)
    return place // 4, place % 4


def chip_index(shift):
    dy, dz = shift
    y, z, _ = head_place()
    return lax.rem(y + (dy + N_Y), N_Y) * N_Z + lax.rem(z + dz, N_Z)


def head_shift(value, dy=0, dz=0, core=0):
    pairs = []
    for i in range(16):
        y, z, c = i // 4, (i // 2) % 2, i % 2
        pairs.append((i, ((y + dy) % 4) * 4 + ((z + dz) % 2) * 2 + (c + core) % 2))
    return lax.ppermute(value, HEAD_AXIS, pairs)


def seq_shift(value, dx=0, dz=0):
    pairs = [(i, ((i // 4 + dz) % 4) * 4 + (i % 4 + dx) % 4) for i in range(16)]
    return lax.ppermute(value, SEQ_AXIS, pairs)


def load(weights, cotangent):
    def body(w_ref, g_ref, o_ref, og_ref, sem):
        copies = [pltpu.make_async_copy(g_ref, og_ref, sem.at[3])]
        copies += [pltpu.make_async_copy(w_ref.at[m], o_ref.at[m], sem.at[m]) for m in range(3)]
        for copy in copies:
            copy.start()
        for copy in copies:
            copy.wait()

    return call(
        body,
        [pltpu.VMEM(weights.shape, BF16), pltpu.VMEM(cotangent.shape, BF16)],
        [pltpu.with_memory_space_constraint(x, pltpu.HBM) for x in (weights, cotangent)],
        [pltpu.SemaphoreType.DMA((4,))],
        moved=2 * weights.size,
        hbm_at=(0, 1),
        limit=4 << 20,
    )


def project(shifts, blocks, weights, total):
    n = len(shifts)
    first = total is None

    def body(*refs):
        refs = list(refs)
        pairs = [(refs.pop(0), refs.pop(0)) for _ in range(n)]
        w_ref = refs.pop(0)
        t_ref = None if first else refs.pop(0)
        o_ref, xcat = refs
        core = head_place()[2]
        for i, (own, other) in enumerate(pairs):
            xcat[i, :, pl.ds(pl.multiple_of(core * BLOCK, BLOCK), BLOCK)] = own[...]
            xcat[i, :, pl.ds(pl.multiple_of((1 - core) * BLOCK, BLOCK), BLOCK)] = other[...]
        for i, shift in enumerate(shifts):
            rows = pl.ds(pl.multiple_of(chip_index(shift) * PAIR, PAIR), PAIR)
            for m in range(3):
                cols = slice(m * COLS, (m + 1) * COLS)
                part = jnp.dot(xcat[i], w_ref[m, rows, :], preferred_element_type=F32)
                if i == 0 and first:
                    o_ref[:, cols] = part
                elif i == 0:
                    o_ref[:, cols] = t_ref[:, cols] + part
                else:
                    o_ref[:, cols] += part

    return call(
        body,
        jax.ShapeDtypeStruct((ROWS, 3 * COLS), F32),
        [b for pair in blocks for b in pair] + [weights] + ([] if first else [total]),
        [pltpu.VMEM((n, ROWS, PAIR), BF16)],
        flops=2 * n * ROWS * PAIR * 3 * COLS,
        moved=n * 3 * PAIR * COLS * 2,
    )


def project_halves(parts, weights, total):
    n = len(parts)

    def body(*refs):
        w_ref, t_ref, o_ref = refs[n:]
        place = head_place()[2]
        for m in range(3):
            cols = slice(m * COLS, (m + 1) * COLS)
            sums = t_ref[:, cols]
            for (shift, own_core, _), x_ref in zip(parts, refs):
                core = place if own_core else 1 - place
                block = chip_index(shift) * 2 + core
                rows = pl.ds(pl.multiple_of(block * BLOCK, BLOCK), BLOCK)
                sums = sums + jnp.dot(
                    x_ref[...], w_ref[m, rows, :], preferred_element_type=F32
                )
            o_ref[:, cols] = sums

    return call(
        body,
        jax.ShapeDtypeStruct((ROWS, 3 * COLS), F32),
        [block for _, _, block in parts] + [weights, total],
        flops=2 * n * ROWS * BLOCK * 3 * COLS,
        moved=n * 3 * BLOCK * COLS * 2,
    )


def decay_matrix(log_decay_row):
    def body(l_ref, o_ref, r_ref):
        i = lax.broadcasted_iota(jnp.int32, (ROWS, ROWS), 0)
        j = lax.broadcasted_iota(jnp.int32, (ROWS, ROWS), 1)
        causal = i >= j
        lower = causal.astype(F32)
        logs = jnp.concatenate([l_ref[...], jnp.zeros((8 - HEADS, ROWS), F32)], axis=0)
        nt = (((1,), (1,)), ((), ()))
        highest = lax.Precision.HIGHEST
        column = lax.dot_general(lower, logs, nt, precision=highest, preferred_element_type=F32)
        row = lax.dot_general(logs, lower, nt, precision=highest, preferred_element_type=F32)
        r_ref[...] = column[:, :HEADS]
        for h in range(HEADS):
            gap = column[:, h : h + 1] - row[h : h + 1, :]
            o_ref[h] = jnp.where(causal, jnp.exp(jnp.where(causal, gap, 0.0)), 0.0) * (
                HEAD**-0.5
            )

    return call(
        body,
        [
            jax.ShapeDtypeStruct((HEADS, ROWS, ROWS), F32),
            jax.ShapeDtypeStruct((ROWS, HEADS), F32),
        ],
        [log_decay_row],
        flops=10 * HEADS * ROWS * ROWS,
        moved=4 * HEADS * ROWS * ROWS,
    )


def local_states(projected, cotangent, running):
    def body(p_ref, g_ref, r_ref, q_ref, k_ref, v_ref, m_ref):
        last = r_ref[ROWS - 1 : ROWS, :]
        for h in range(HEADS):
            cols = slice(h * HEAD, (h + 1) * HEAD)
            query = jax.nn.silu(p_ref[:, cols]).astype(BF16)
            key = jax.nn.silu(p_ref[:, COLS + h * HEAD : COLS + (h + 1) * HEAD]).astype(BF16)
            value = p_ref[:, 2 * COLS + h * HEAD : 2 * COLS + (h + 1) * HEAD].astype(BF16)
            q_ref[:, cols], k_ref[:, cols], v_ref[:, cols] = query, key, value
            run = r_ref[:, h : h + 1]
            fall = jnp.exp(last[:, h : h + 1] - run)
            rise = jnp.exp(run)
            tn = (((0,), (0,)), ((), ()))
            key_state = lax.dot_general(
                (key.astype(F32) * fall).astype(BF16), value, tn, preferred_element_type=F32
            )
            query_state = lax.dot_general(
                (query.astype(F32) * rise).astype(BF16),
                g_ref[:, cols],
                tn,
                preferred_element_type=F32,
            )
            m_ref[h * HEAD : (h + 1) * HEAD, :] = key_state.astype(BF16)
            m_ref[COLS + h * HEAD : COLS + (h + 1) * HEAD, :] = query_state.astype(BF16)
        header(m_ref, 2 * COLS, [last[:, h : h + 1] for h in range(HEADS)])

    act = jax.ShapeDtypeStruct((ROWS, COLS), BF16)
    return call(
        body,
        [act, act, act, jax.ShapeDtypeStruct((2 * COLS + HDR, HEAD), BF16)],
        [projected, cotangent, running],
        flops=8 * ROWS * HEAD * COLS,
        moved=ROWS * COLS * 16,
    )


def header(ref, row, totals):
    sub = lax.broadcasted_iota(jnp.int32, (HDR, HEAD), 0)
    block = jnp.zeros((HDR, HEAD), F32)
    for h in range(HEADS):
        total = jnp.broadcast_to(totals[h], (HDR, HEAD))
        high = total.astype(BF16).astype(F32)
        block = jnp.where(sub == h, high, block)
        block = jnp.where(sub == HEADS + h, total - high, block)
    ref[row : row + HDR, :] = block.astype(BF16)


def read_totals(ref, row):
    block = ref[row : row + HDR, :].astype(F32)
    return [block[h : h + 1, :] + block[HEADS + h : HEADS + h + 1, :] for h in range(HEADS)]


def inner_part(query, key, value, cotangent, decays):
    def body(q_ref, k_ref, v_ref, g_ref, d_ref, gq_ref, gk_ref, gv_ref):
        nt = (((1,), (1,)), ((), ()))
        tn = (((0,), (0,)), ((), ()))
        for h in range(HEADS):
            cols = slice(h * HEAD, (h + 1) * HEAD)
            q, k, v, g = q_ref[:, cols], k_ref[:, cols], v_ref[:, cols], g_ref[:, cols]
            decay = d_ref[h]
            out_value = (
                lax.dot_general(g, v, nt, preferred_element_type=F32) * decay
            ).astype(BF16)
            query_key = (
                lax.dot_general(q, k, nt, preferred_element_type=F32) * decay
            ).astype(BF16)
            gq_ref[:, cols] = jnp.dot(out_value, k, preferred_element_type=F32)
            gk_ref[:, cols] = lax.dot_general(out_value, q, tn, preferred_element_type=F32)
            gv_ref[:, cols] = lax.dot_general(query_key, g, tn, preferred_element_type=F32)

    part = jax.ShapeDtypeStruct((ROWS, COLS), F32)
    return call(
        body,
        [part] * 3,
        [query, key, value, cotangent, decays],
        flops=10 * ROWS * ROWS * COLS,
        moved=ROWS * COLS * 20,
    )


def join_x(own, received):
    def body(own_ref, *refs):
        got = refs[:3]
        send = refs[3:6]
        keep_ref, scale_ref = refs[6:]
        z, x = seq_place()
        messages = [own_ref] + list(got)
        row = 2 * COLS
        totals = [read_totals(m, row) for m in messages]
        source = [lax.rem(x - s + N_X, N_X) for s in range(N_X)]
        for h in range(HEADS):
            zero = jnp.zeros((1, HEAD), F32)

            def between(low, high):
                out = zero
                for s in range(N_X):
                    inside = jnp.logical_and(source[s] > low, source[s] < high)
                    out = out + jnp.where(inside, totals[s][h], 0.0)
                return out

            key_all = jnp.zeros((HEAD, HEAD), F32)
            query_all = jnp.zeros((HEAD, HEAD), F32)
            key_before = jnp.zeros((HEAD, HEAD), F32)
            query_after = jnp.zeros((HEAD, HEAD), F32)
            for s in range(N_X):
                ks = messages[s][h * HEAD : (h + 1) * HEAD, :].astype(F32)
                qs = messages[s][COLS + h * HEAD : COLS + (h + 1) * HEAD, :].astype(F32)
                p = source[s]
                key_all += jnp.exp(between(p, N_X)) * ks
                query_all += jnp.exp(between(-1, p)) * qs
                if s:
                    key_before += jnp.where(p < x, jnp.exp(between(p, x)), 0.0) * ks
                    query_after += jnp.where(p > x, jnp.exp(between(x, p)), 0.0) * qs
            rows = slice(h * HEAD, (h + 1) * HEAD)
            keep_ref[rows, :] = key_before
            keep_ref[COLS + h * HEAD : COLS + (h + 1) * HEAD, :] = query_after
            scale_ref[h : h + 1, :] = jnp.exp(between(-1, x))
            scale_ref[HEADS + h : HEADS + h + 1, :] = jnp.exp(between(x, N_X))
            for s in range(1, N_ZHI):
                later = jnp.full((HEAD, HEAD), z + s) < N_ZHI
                send[s - 1][rows, :] = jnp.where(later, key_all, query_all).astype(BF16)
        group = [sum(totals[s][h] for s in range(N_X)) for h in range(HEADS)]
        for s in range(1, N_ZHI):
            header(send[s - 1], COLS, group)

    message = jax.ShapeDtypeStruct((COLS + HDR, HEAD), BF16)
    return call(
        body,
        [message] * 3
        + [jax.ShapeDtypeStruct((2 * COLS, HEAD), F32), jax.ShapeDtypeStruct((8, HEAD), F32)],
        [own] + list(received),
        flops=40 * COLS * HEAD,
        moved=COLS * HEAD * 20,
    )


def outer_part(received, keep, scale, projected, act, cotangent, inner, running):
    def body(*refs):
        got = refs[:3]
        keep_ref, scale_ref, p_ref, _, k_ref, v_ref, g_ref = refs[3:10]
        gq_ref, gk_ref, gv_ref, r_ref, o_ref = refs[10:]
        z, _ = seq_place()
        nt = (((1,), (1,)), ((), ()))
        source = [lax.rem(z - s + N_ZHI, N_ZHI) for s in range(1, N_ZHI)]
        totals = [read_totals(m, COLS) for m in got]
        c = HEAD**-0.5
        last = r_ref[ROWS - 1 : ROWS, :]

        def slope(v):
            s = jax.nn.sigmoid(v)
            return s * (1.0 + v * (1.0 - s))

        for h in range(HEADS):
            cols = slice(h * HEAD, (h + 1) * HEAD)

            def between(low, high):
                out = jnp.zeros((1, HEAD), F32)
                for s in range(N_ZHI - 1):
                    inside = jnp.logical_and(source[s] > low, source[s] < high)
                    out = out + jnp.where(inside, totals[s][h], 0.0)
                return out

            before = jnp.zeros((HEAD, HEAD), F32)
            after = jnp.zeros((HEAD, HEAD), F32)
            for s in range(N_ZHI - 1):
                p = source[s]
                state = got[s][cols, :].astype(F32)
                before += jnp.where(p < z, jnp.exp(between(p, z)), 0.0) * state
                after += jnp.where(p > z, jnp.exp(between(z, p)), 0.0) * state
            state_in = (keep_ref[cols, :] + scale_ref[h : h + 1, :] * before).astype(BF16)
            grad_in = (
                keep_ref[COLS + h * HEAD : COLS + (h + 1) * HEAD, :]
                + scale_ref[HEADS + h : HEADS + h + 1, :] * after
            ).astype(BF16)
            run = r_ref[:, h : h + 1]
            rise = jnp.exp(run) * c
            fall = jnp.exp(last[:, h : h + 1] - run) * c
            grad_query = gq_ref[:, cols] + rise * lax.dot_general(
                g_ref[:, cols], state_in, nt, preferred_element_type=F32
            )
            grad_key = gk_ref[:, cols] + fall * lax.dot_general(
                v_ref[:, cols], grad_in, nt, preferred_element_type=F32
            )
            grad_value = gv_ref[:, cols] + fall * jnp.dot(
                k_ref[:, cols], grad_in, preferred_element_type=F32
            )
            grads = (
                grad_query * slope(p_ref[:, cols]),
                grad_key * slope(p_ref[:, COLS + h * HEAD : COLS + (h + 1) * HEAD]),
                grad_value,
            )
            for m in range(3):
                at = m * COLS + h * HEAD
                o_ref[at : at + HEAD, :] = grads[m].T.astype(BF16)

    return call(
        body,
        jax.ShapeDtypeStruct((3 * COLS, ROWS), BF16),
        list(received) + [keep, scale, projected] + list(act) + [cotangent] + list(inner) + [running],
        flops=6 * ROWS * HEAD * COLS,
        moved=ROWS * COLS * 40,
    )


def partials(shifts, grads, weights, received, own_core, dtype=BF16):
    n = len(shifts)
    add = received is not None

    def body(*refs):
        refs = list(refs)
        g_ref, w_ref = refs.pop(0), refs.pop(0)
        r_ref = refs.pop(0) if add else None
        outs = refs
        core = head_place()[2]
        if not own_core:
            core = 1 - core
        for i, shift in enumerate(shifts):
            block = chip_index(shift) * 2 + core
            rows = pl.ds(pl.multiple_of(block * BLOCK, BLOCK), BLOCK)
            part = None
            for m in range(3):
                term = jnp.dot(
                    w_ref[m, rows, :],
                    g_ref[m * COLS : (m + 1) * COLS, :],
                    preferred_element_type=F32,
                )
                part = term if part is None else part + term
            if add:
                outs[i][...] = (part + r_ref[i].astype(F32)).astype(BF16)
            else:
                outs[0][i] = part.astype(dtype)

    block = jax.ShapeDtypeStruct((BLOCK, ROWS), BF16)
    return call(
        body,
        [block] * n if add else [jax.ShapeDtypeStruct((n, BLOCK, ROWS), dtype)],
        [grads, weights] + ([received] if add else []),
        flops=2 * n * ROWS * BLOCK * 3 * COLS,
        moved=n * 3 * BLOCK * COLS * 2,
    )


def add_cores(own, received):
    def body(a_ref, b_ref, *outs):
        for i, out in enumerate(outs):
            out[...] = (a_ref[i] + b_ref[i].astype(F32)).astype(BF16)

    n = own.shape[0]
    return call(
        body,
        [jax.ShapeDtypeStruct((BLOCK, ROWS), BF16)] * n,
        [own, received],
        flops=n * BLOCK * ROWS,
        moved=n * BLOCK * ROWS * 8,
    )


def add_all(parts):
    def body(*refs):
        total = refs[0][...].astype(F32)
        for ref in refs[1:-1]:
            total = total + ref[...].astype(F32)
        refs[-1][...] = total.astype(BF16)

    return call(
        body,
        jax.ShapeDtypeStruct((BLOCK, ROWS), BF16),
        list(parts),
        flops=len(parts) * BLOCK * ROWS,
        moved=BLOCK * ROWS * 2 * (len(parts) + 1),
    )


def finish(parts):
    def body(*refs):
        total = refs[0][...].astype(F32)
        for ref in refs[1:-1]:
            total = total + ref[...].astype(F32)
        refs[-1][...] = total.T.astype(BF16)

    return call(
        body,
        jax.ShapeDtypeStruct((ROWS, BLOCK), BF16),
        list(parts),
        flops=5 * BLOCK * ROWS,
        moved=BLOCK * ROWS * 12,
    )


OWN, FAR, UP, DOWN = (0, 0), (2, 0), (-1, 0), (1, 0)
SIDE, FAR_SIDE, UP_SIDE, DOWN_SIDE = (0, 1), (2, 1), (-1, 1), (1, 1)
GROUPS = (
    ((DOWN_SIDE,), True),
    ((FAR_SIDE,), True),
    ((UP_SIDE, FAR), True),
    ((DOWN, UP), False),
    ((SIDE, OWN), False),
)


def layer(inputs, weights, cotangent, log_decay):
    decays, running = decay_matrix(log_decay.T)

    side = head_shift(inputs, dz=1)
    up = head_shift(inputs, dy=1)
    down = head_shift(inputs, dy=-1)
    far = head_shift(inputs, dy=2)
    up_side = head_shift(up, dz=1)
    far_side = head_shift(side, dy=2)
    down_side = head_shift(down, dz=1)

    def both(block):
        return (block, head_shift(block, core=1))

    resident, cotangent = load(weights, cotangent)
    total = project([OWN], [both(inputs)], resident, None)
    total = project([UP, SIDE, DOWN], [both(up), both(side), both(down)], resident, total)
    total = project([FAR], [both(far)], resident, total)
    total = project([UP_SIDE], [both(up_side)], resident, total)
    _, far_other = both(far_side)
    _, down_other = both(down_side)
    total = project_halves([(FAR_SIDE, True, far_side)], resident, total)
    total = project_halves(
        [(FAR_SIDE, False, far_other), (DOWN_SIDE, True, down_side)], resident, total
    )
    total = project_halves([(DOWN_SIDE, False, down_other)], resident, total)

    query, key, value, message = local_states(total, cotangent, running)
    over_x = [seq_shift(message, dx=s) for s in (1, 2, 3)]
    inner = inner_part(query, key, value, cotangent, decays)
    *send, keep, scale = join_x(message, over_x)
    over_z = [seq_shift(send[s - 1], dz=s) for s in (1, 2, 3)]
    grads = outer_part(
        over_z, keep, scale, total, (query, key, value), cotangent, inner, running
    )

    blocks = {}
    for group, apart in GROUPS:
        (share,) = partials(group, grads, resident, None, False)
        got = head_shift(share, core=1)
        if apart:
            (own,) = partials(group, grads, resident, None, True, F32)
            done = add_cores(own, got)
        else:
            done = partials(group, grads, resident, got, True)
        blocks.update(zip(group, done))
    down_side = head_shift(blocks[DOWN_SIDE], dz=1)
    far_side = head_shift(blocks[FAR_SIDE], dy=2)
    up_side = head_shift(blocks[UP_SIDE], dz=1)
    far = head_shift(blocks[FAR], dy=2)
    down = head_shift(add_all([blocks[DOWN], down_side]), dy=1)
    side = head_shift(add_all([blocks[SIDE], far_side]), dz=1)
    up = head_shift(add_all([blocks[UP], up_side]), dy=-1)
    return finish([blocks[OWN], far, down, up, side])


def solution(mesh):
    rows = P(SEQ_AXIS, HEAD_AXIS)
    return jax.shard_map(
        layer,
        mesh=mesh,
        in_specs=(rows, P(None, None, HEAD_AXIS), rows, rows),
        out_specs=rows,
        check_vma=False,
    )
```

```python
import jax
import jax.numpy as jnp
from jax import lax
from jax.experimental import pallas as pl
from jax.experimental.pallas import tpu as pltpu
from jax.sharding import PartitionSpec as P


SEQ_AXIS, HEAD_AXIS = "seq", "head"
F32 = jnp.float32
BF16 = jnp.bfloat16
ROWS = 384
HEAD = 128
HEADS = 2
COLS = HEADS * HEAD
BLOCK = 384
PAIR = 2 * BLOCK
N_Y, N_Z = 4, 2
N_X, N_ZHI = 4, 4
HDR = 16
VMEM = pl.BlockSpec(memory_space=pltpu.VMEM)
HBM = pl.BlockSpec(memory_space=pltpu.HBM)


def call(body, outs, ins, scratch=(), flops=0, moved=0, hbm_at=(), limit=8 << 20):
    specs = [HBM if i in hbm_at else VMEM for i in range(len(ins))]
    single = not isinstance(outs, (list, tuple))
    return pl.pallas_call(
        body,
        out_shape=outs,
        in_specs=specs,
        out_specs=VMEM if single else [VMEM] * len(outs),
        scratch_shapes=list(scratch),
        compiler_params=pltpu.CompilerParams(vmem_limit_bytes=limit),
        cost_estimate=pl.CostEstimate(flops=flops, bytes_accessed=moved, transcendentals=0),
    )(*ins)


def head_place():
    place = lax.axis_index(HEAD_AXIS)
    return place // 4, (place // 2) % 2, place % 2


def seq_place():
    place = lax.axis_index(SEQ_AXIS)
    return place // 4, place % 4


def chip_index(shift):
    dy, dz = shift
    y, z, _ = head_place()
    return lax.rem(y + (dy + N_Y), N_Y) * N_Z + lax.rem(z + dz, N_Z)


def head_shift(value, dy=0, dz=0, core=0):
    pairs = []
    for i in range(16):
        y, z, c = i // 4, (i // 2) % 2, i % 2
        pairs.append((i, ((y + dy) % 4) * 4 + ((z + dz) % 2) * 2 + (c + core) % 2))
    return lax.ppermute(value, HEAD_AXIS, pairs)


def seq_shift(value, dx=0, dz=0):
    pairs = [(i, ((i // 4 + dz) % 4) * 4 + (i % 4 + dx) % 4) for i in range(16)]
    return lax.ppermute(value, SEQ_AXIS, pairs)


def load(weights, cotangent):
    def body(w_ref, g_ref, o_ref, og_ref, sem):
        copies = [pltpu.make_async_copy(g_ref, og_ref, sem.at[3])]
        copies += [pltpu.make_async_copy(w_ref.at[m], o_ref.at[m], sem.at[m]) for m in range(3)]
        for copy in copies:
            copy.start()
        for copy in copies:
            copy.wait()

    return call(
        body,
        [pltpu.VMEM(weights.shape, BF16), pltpu.VMEM(cotangent.shape, BF16)],
        [pltpu.with_memory_space_constraint(x, pltpu.HBM) for x in (weights, cotangent)],
        [pltpu.SemaphoreType.DMA((4,))],
        moved=2 * weights.size,
        hbm_at=(0, 1),
        limit=4 << 20,
    )


def project(shifts, blocks, weights, total):
    n = len(shifts)
    first = total is None

    def body(*refs):
        refs = list(refs)
        pairs = [tuple([refs.pop(0) for _ in part] for part in pair) for pair in blocks]
        w_ref = refs.pop(0)
        t_ref = None if first else refs.pop(0)
        o_ref, xcat = refs
        core = head_place()[2]
        for i, (own, other) in enumerate(pairs):
            for pieces, place in ((own, core), (other, 1 - core)):
                row = 0
                for piece in pieces:
                    height = piece.shape[0]
                    cols = pl.ds(pl.multiple_of(place * BLOCK, BLOCK), BLOCK)
                    xcat[i, row : row + height, cols] = piece[...]
                    row += height
        for i, shift in enumerate(shifts):
            rows = pl.ds(pl.multiple_of(chip_index(shift) * PAIR, PAIR), PAIR)
            for m in range(3):
                cols = slice(m * COLS, (m + 1) * COLS)
                part = jnp.dot(xcat[i], w_ref[m, rows, :], preferred_element_type=F32)
                if i == 0 and first:
                    o_ref[:, cols] = part
                elif i == 0:
                    o_ref[:, cols] = t_ref[:, cols] + part
                else:
                    o_ref[:, cols] += part

    return call(
        body,
        jax.ShapeDtypeStruct((ROWS, 3 * COLS), F32),
        [piece for pair in blocks for part in pair for piece in part] + [weights] + ([] if first else [total]),
        [pltpu.VMEM((n, ROWS, PAIR), BF16)],
        flops=2 * n * ROWS * PAIR * 3 * COLS,
        moved=n * 3 * PAIR * COLS * 2,
    )


def split(first, second):
    half = ROWS // 2

    def body(a_ref, b_ref, upper, lower):
        upper[...] = a_ref[:half, :]
        lower[...] = b_ref[half:, :]

    return call(
        body,
        [jax.ShapeDtypeStruct((half, BLOCK), BF16)] * 2,
        [first, second],
        moved=4 * half * BLOCK * 2,
    )


def project_halves(parts, weights, total):
    n = len(parts)

    def body(*refs):
        w_ref, t_ref, o_ref = refs[n:]
        place = head_place()[2]
        for m in range(3):
            cols = slice(m * COLS, (m + 1) * COLS)
            sums = t_ref[:, cols]
            for (shift, own_core, _), x_ref in zip(parts, refs):
                core = place if own_core else 1 - place
                block = chip_index(shift) * 2 + core
                rows = pl.ds(pl.multiple_of(block * BLOCK, BLOCK), BLOCK)
                sums = sums + jnp.dot(
                    x_ref[...], w_ref[m, rows, :], preferred_element_type=F32
                )
            o_ref[:, cols] = sums

    return call(
        body,
        jax.ShapeDtypeStruct((ROWS, 3 * COLS), F32),
        [block for _, _, block in parts] + [weights, total],
        flops=2 * n * ROWS * BLOCK * 3 * COLS,
        moved=n * 3 * BLOCK * COLS * 2,
    )


def decay_matrix(log_decay_row):
    def body(l_ref, o_ref, r_ref):
        i = lax.broadcasted_iota(jnp.int32, (ROWS, ROWS), 0)
        j = lax.broadcasted_iota(jnp.int32, (ROWS, ROWS), 1)
        causal = i >= j
        lower = causal.astype(F32)
        logs = jnp.concatenate([l_ref[...], jnp.zeros((8 - HEADS, ROWS), F32)], axis=0)
        nt = (((1,), (1,)), ((), ()))
        highest = lax.Precision.HIGHEST
        column = lax.dot_general(lower, logs, nt, precision=highest, preferred_element_type=F32)
        row = lax.dot_general(logs, lower, nt, precision=highest, preferred_element_type=F32)
        r_ref[...] = column[:, :HEADS]
        for h in range(HEADS):
            gap = column[:, h : h + 1] - row[h : h + 1, :]
            o_ref[h] = jnp.where(causal, jnp.exp(jnp.where(causal, gap, 0.0)), 0.0) * (
                HEAD**-0.5
            )

    return call(
        body,
        [
            jax.ShapeDtypeStruct((HEADS, ROWS, ROWS), F32),
            jax.ShapeDtypeStruct((ROWS, HEADS), F32),
        ],
        [log_decay_row],
        flops=10 * HEADS * ROWS * ROWS,
        moved=4 * HEADS * ROWS * ROWS,
    )


def local_states(projected, cotangent, running):
    def body(p_ref, g_ref, r_ref, q_ref, k_ref, v_ref, m_ref):
        last = r_ref[ROWS - 1 : ROWS, :]
        for h in range(HEADS):
            cols = slice(h * HEAD, (h + 1) * HEAD)
            query = jax.nn.silu(p_ref[:, cols]).astype(BF16)
            key = jax.nn.silu(p_ref[:, COLS + h * HEAD : COLS + (h + 1) * HEAD]).astype(BF16)
            value = p_ref[:, 2 * COLS + h * HEAD : 2 * COLS + (h + 1) * HEAD].astype(BF16)
            q_ref[:, cols], k_ref[:, cols], v_ref[:, cols] = query, key, value
            run = r_ref[:, h : h + 1]
            fall = jnp.exp(last[:, h : h + 1] - run)
            rise = jnp.exp(run)
            tn = (((0,), (0,)), ((), ()))
            key_state = lax.dot_general(
                (key.astype(F32) * fall).astype(BF16), value, tn, preferred_element_type=F32
            )
            query_state = lax.dot_general(
                (query.astype(F32) * rise).astype(BF16),
                g_ref[:, cols],
                tn,
                preferred_element_type=F32,
            )
            m_ref[h * HEAD : (h + 1) * HEAD, :] = key_state.astype(BF16)
            m_ref[COLS + h * HEAD : COLS + (h + 1) * HEAD, :] = query_state.astype(BF16)
        header(m_ref, 2 * COLS, [last[:, h : h + 1] for h in range(HEADS)])

    act = jax.ShapeDtypeStruct((ROWS, COLS), BF16)
    return call(
        body,
        [act, act, act, jax.ShapeDtypeStruct((2 * COLS + HDR, HEAD), BF16)],
        [projected, cotangent, running],
        flops=8 * ROWS * HEAD * COLS,
        moved=ROWS * COLS * 16,
    )


def header(ref, row, totals):
    sub = lax.broadcasted_iota(jnp.int32, (HDR, HEAD), 0)
    block = jnp.zeros((HDR, HEAD), F32)
    for h in range(HEADS):
        total = jnp.broadcast_to(totals[h], (HDR, HEAD))
        high = total.astype(BF16).astype(F32)
        block = jnp.where(sub == h, high, block)
        block = jnp.where(sub == HEADS + h, total - high, block)
    ref[row : row + HDR, :] = block.astype(BF16)


def read_totals(ref, row):
    block = ref[row : row + HDR, :].astype(F32)
    return [block[h : h + 1, :] + block[HEADS + h : HEADS + h + 1, :] for h in range(HEADS)]


def inner_part(query, key, value, cotangent, decays):
    def body(q_ref, k_ref, v_ref, g_ref, d_ref, gq_ref, gk_ref, gv_ref):
        nt = (((1,), (1,)), ((), ()))
        tn = (((0,), (0,)), ((), ()))
        for h in range(HEADS):
            cols = slice(h * HEAD, (h + 1) * HEAD)
            q, k, v, g = q_ref[:, cols], k_ref[:, cols], v_ref[:, cols], g_ref[:, cols]
            decay = d_ref[h]
            out_value = (
                lax.dot_general(g, v, nt, preferred_element_type=F32) * decay
            ).astype(BF16)
            query_key = (
                lax.dot_general(q, k, nt, preferred_element_type=F32) * decay
            ).astype(BF16)
            gq_ref[:, cols] = jnp.dot(out_value, k, preferred_element_type=F32)
            gk_ref[:, cols] = lax.dot_general(out_value, q, tn, preferred_element_type=F32)
            gv_ref[:, cols] = lax.dot_general(query_key, g, tn, preferred_element_type=F32)

    part = jax.ShapeDtypeStruct((ROWS, COLS), F32)
    return call(
        body,
        [part] * 3,
        [query, key, value, cotangent, decays],
        flops=10 * ROWS * ROWS * COLS,
        moved=ROWS * COLS * 20,
    )


def join_x(own, received):
    def body(own_ref, *refs):
        got = refs[:3]
        send = refs[3:6]
        keep_ref, scale_ref = refs[6:]
        z, x = seq_place()
        messages = [own_ref] + list(got)
        row = 2 * COLS
        totals = [read_totals(m, row) for m in messages]
        source = [lax.rem(x - s + N_X, N_X) for s in range(N_X)]
        for h in range(HEADS):
            zero = jnp.zeros((1, HEAD), F32)

            def between(low, high):
                out = zero
                for s in range(N_X):
                    inside = jnp.logical_and(source[s] > low, source[s] < high)
                    out = out + jnp.where(inside, totals[s][h], 0.0)
                return out

            key_all = jnp.zeros((HEAD, HEAD), F32)
            query_all = jnp.zeros((HEAD, HEAD), F32)
            key_before = jnp.zeros((HEAD, HEAD), F32)
            query_after = jnp.zeros((HEAD, HEAD), F32)
            for s in range(N_X):
                ks = messages[s][h * HEAD : (h + 1) * HEAD, :].astype(F32)
                qs = messages[s][COLS + h * HEAD : COLS + (h + 1) * HEAD, :].astype(F32)
                p = source[s]
                key_all += jnp.exp(between(p, N_X)) * ks
                query_all += jnp.exp(between(-1, p)) * qs
                if s:
                    key_before += jnp.where(p < x, jnp.exp(between(p, x)), 0.0) * ks
                    query_after += jnp.where(p > x, jnp.exp(between(x, p)), 0.0) * qs
            rows = slice(h * HEAD, (h + 1) * HEAD)
            keep_ref[rows, :] = key_before
            keep_ref[COLS + h * HEAD : COLS + (h + 1) * HEAD, :] = query_after
            scale_ref[h : h + 1, :] = jnp.exp(between(-1, x))
            scale_ref[HEADS + h : HEADS + h + 1, :] = jnp.exp(between(x, N_X))
            for s in range(1, N_ZHI):
                later = jnp.full((HEAD, HEAD), z + s) < N_ZHI
                send[s - 1][rows, :] = jnp.where(later, key_all, query_all).astype(BF16)
        group = [sum(totals[s][h] for s in range(N_X)) for h in range(HEADS)]
        for s in range(1, N_ZHI):
            header(send[s - 1], COLS, group)

    message = jax.ShapeDtypeStruct((COLS + HDR, HEAD), BF16)
    return call(
        body,
        [message] * 3
        + [jax.ShapeDtypeStruct((2 * COLS, HEAD), F32), jax.ShapeDtypeStruct((8, HEAD), F32)],
        [own] + list(received),
        flops=40 * COLS * HEAD,
        moved=COLS * HEAD * 20,
    )


def outer_part(received, keep, scale, projected, act, cotangent, inner, running):
    def body(*refs):
        got = refs[:3]
        keep_ref, scale_ref, p_ref, _, k_ref, v_ref, g_ref = refs[3:10]
        gq_ref, gk_ref, gv_ref, r_ref, o_ref = refs[10:]
        z, _ = seq_place()
        nt = (((1,), (1,)), ((), ()))
        source = [lax.rem(z - s + N_ZHI, N_ZHI) for s in range(1, N_ZHI)]
        totals = [read_totals(m, COLS) for m in got]
        c = HEAD**-0.5
        last = r_ref[ROWS - 1 : ROWS, :]

        def slope(v):
            s = jax.nn.sigmoid(v)
            return s * (1.0 + v * (1.0 - s))

        for h in range(HEADS):
            cols = slice(h * HEAD, (h + 1) * HEAD)

            def between(low, high):
                out = jnp.zeros((1, HEAD), F32)
                for s in range(N_ZHI - 1):
                    inside = jnp.logical_and(source[s] > low, source[s] < high)
                    out = out + jnp.where(inside, totals[s][h], 0.0)
                return out

            before = jnp.zeros((HEAD, HEAD), F32)
            after = jnp.zeros((HEAD, HEAD), F32)
            for s in range(N_ZHI - 1):
                p = source[s]
                state = got[s][cols, :].astype(F32)
                before += jnp.where(p < z, jnp.exp(between(p, z)), 0.0) * state
                after += jnp.where(p > z, jnp.exp(between(z, p)), 0.0) * state
            state_in = (keep_ref[cols, :] + scale_ref[h : h + 1, :] * before).astype(BF16)
            grad_in = (
                keep_ref[COLS + h * HEAD : COLS + (h + 1) * HEAD, :]
                + scale_ref[HEADS + h : HEADS + h + 1, :] * after
            ).astype(BF16)
            run = r_ref[:, h : h + 1]
            rise = jnp.exp(run) * c
            fall = jnp.exp(last[:, h : h + 1] - run) * c
            grad_query = gq_ref[:, cols] + rise * lax.dot_general(
                g_ref[:, cols], state_in, nt, preferred_element_type=F32
            )
            grad_key = gk_ref[:, cols] + fall * lax.dot_general(
                v_ref[:, cols], grad_in, nt, preferred_element_type=F32
            )
            grad_value = gv_ref[:, cols] + fall * jnp.dot(
                k_ref[:, cols], grad_in, preferred_element_type=F32
            )
            grads = (
                grad_query * slope(p_ref[:, cols]),
                grad_key * slope(p_ref[:, COLS + h * HEAD : COLS + (h + 1) * HEAD]),
                grad_value,
            )
            for m in range(3):
                at = m * COLS + h * HEAD
                o_ref[at : at + HEAD, :] = grads[m].T.astype(BF16)

    return call(
        body,
        jax.ShapeDtypeStruct((3 * COLS, ROWS), BF16),
        list(received) + [keep, scale, projected] + list(act) + [cotangent] + list(inner) + [running],
        flops=6 * ROWS * HEAD * COLS,
        moved=ROWS * COLS * 40,
    )


def partials(shifts, grads, weights, received, own_core, dtype=BF16):
    n = len(shifts)
    add = received is not None

    def body(*refs):
        refs = list(refs)
        g_ref, w_ref = refs.pop(0), refs.pop(0)
        r_ref = refs.pop(0) if add else None
        outs = refs
        core = head_place()[2]
        if not own_core:
            core = 1 - core
        for i, shift in enumerate(shifts):
            block = chip_index(shift) * 2 + core
            rows = pl.ds(pl.multiple_of(block * BLOCK, BLOCK), BLOCK)
            part = None
            for m in range(3):
                term = jnp.dot(
                    w_ref[m, rows, :],
                    g_ref[m * COLS : (m + 1) * COLS, :],
                    preferred_element_type=F32,
                )
                part = term if part is None else part + term
            if add:
                outs[i][...] = (part + r_ref[i].astype(F32)).astype(BF16)
            else:
                outs[0][i] = part.astype(dtype)

    block = jax.ShapeDtypeStruct((BLOCK, ROWS), BF16)
    return call(
        body,
        [block] * n if add else [jax.ShapeDtypeStruct((n, BLOCK, ROWS), dtype)],
        [grads, weights] + ([received] if add else []),
        flops=2 * n * ROWS * BLOCK * 3 * COLS,
        moved=n * 3 * BLOCK * COLS * 2,
    )


def add_cores(own, received):
    def body(a_ref, b_ref, *outs):
        for i, out in enumerate(outs):
            out[...] = (a_ref[i] + b_ref[i].astype(F32)).astype(BF16)

    n = own.shape[0]
    return call(
        body,
        [jax.ShapeDtypeStruct((BLOCK, ROWS), BF16)] * n,
        [own, received],
        flops=n * BLOCK * ROWS,
        moved=n * BLOCK * ROWS * 8,
    )


def add_all(parts):
    def body(*refs):
        total = refs[0][...].astype(F32)
        for ref in refs[1:-1]:
            total = total + ref[...].astype(F32)
        refs[-1][...] = total.astype(BF16)

    return call(
        body,
        jax.ShapeDtypeStruct((BLOCK, ROWS), BF16),
        list(parts),
        flops=len(parts) * BLOCK * ROWS,
        moved=BLOCK * ROWS * 2 * (len(parts) + 1),
    )


def finish(parts):
    def body(*refs):
        total = refs[0][...].astype(F32)
        for ref in refs[1:-1]:
            total = total + ref[...].astype(F32)
        refs[-1][...] = total.T.astype(BF16)

    return call(
        body,
        jax.ShapeDtypeStruct((ROWS, BLOCK), BF16),
        list(parts),
        flops=5 * BLOCK * ROWS,
        moved=BLOCK * ROWS * 12,
    )


OWN, FAR, UP, DOWN = (0, 0), (2, 0), (-1, 0), (1, 0)
SIDE, FAR_SIDE, UP_SIDE, DOWN_SIDE = (0, 1), (2, 1), (-1, 1), (1, 1)
GROUPS = (
    ((DOWN_SIDE,), True),
    ((FAR_SIDE,), True),
    ((UP_SIDE, FAR), True),
    ((DOWN, UP), False),
    ((SIDE, OWN), False),
)


def layer(inputs, weights, cotangent, log_decay):
    decays, running = decay_matrix(log_decay.T)

    side = head_shift(inputs, dz=1)
    up = head_shift(inputs, dy=1)
    down = head_shift(inputs, dy=-1)
    upper, lower = split(up, down)
    upper = head_shift(upper, dy=1)
    lower = head_shift(lower, dy=-1)
    up_side = head_shift(up, dz=1)
    far_side = head_shift(side, dy=2)
    down_side = head_shift(down, dz=1)

    def both(block):
        return ([block], [head_shift(block, core=1)])

    resident, cotangent = load(weights, cotangent)
    total = project([OWN], [both(inputs)], resident, None)
    total = project([UP, SIDE, DOWN], [both(up), both(side), both(down)], resident, total)
    total = project([UP_SIDE], [both(up_side)], resident, total)
    (_, [upper_other]), (_, [lower_other]) = both(upper), both(lower)
    total = project([FAR], [([upper, lower], [upper_other, lower_other])], resident, total)
    _, [far_other] = both(far_side)
    _, [down_other] = both(down_side)
    total = project_halves([(FAR_SIDE, True, far_side)], resident, total)
    total = project_halves(
        [(FAR_SIDE, False, far_other), (DOWN_SIDE, True, down_side)], resident, total
    )
    total = project_halves([(DOWN_SIDE, False, down_other)], resident, total)

    query, key, value, message = local_states(total, cotangent, running)
    over_x = [seq_shift(message, dx=s) for s in (1, 2, 3)]
    inner = inner_part(query, key, value, cotangent, decays)
    *send, keep, scale = join_x(message, over_x)
    over_z = [seq_shift(send[s - 1], dz=s) for s in (1, 2, 3)]
    grads = outer_part(
        over_z, keep, scale, total, (query, key, value), cotangent, inner, running
    )

    blocks = {}
    for group, apart in GROUPS:
        (share,) = partials(group, grads, resident, None, False)
        got = head_shift(share, core=1)
        if apart:
            (own,) = partials(group, grads, resident, None, True, F32)
            done = add_cores(own, got)
        else:
            done = partials(group, grads, resident, got, True)
        blocks.update(zip(group, done))
    down_side = head_shift(blocks[DOWN_SIDE], dz=1)
    far_side = head_shift(blocks[FAR_SIDE], dy=2)
    up_side = head_shift(blocks[UP_SIDE], dz=1)
    far = head_shift(blocks[FAR], dy=2)
    down = head_shift(add_all([blocks[DOWN], down_side]), dy=1)
    side = head_shift(add_all([blocks[SIDE], far_side]), dz=1)
    up = head_shift(add_all([blocks[UP], up_side]), dy=-1)
    return finish([blocks[OWN], far, down, up, side])


def solution(mesh):
    rows = P(SEQ_AXIS, HEAD_AXIS)
    return jax.shard_map(
        layer,
        mesh=mesh,
        in_specs=(rows, P(None, None, HEAD_AXIS), rows, rows),
        out_specs=rows,
        check_vma=False,
    )
```

```python
import jax
import jax.numpy as jnp
from jax import lax
from jax.experimental import pallas as pl
from jax.experimental.pallas import tpu as pltpu
from jax.sharding import PartitionSpec as P


SEQ_AXIS, HEAD_AXIS = "seq", "head"
F32 = jnp.float32
BF16 = jnp.bfloat16
ROWS = 384
HEAD = 128
HEADS = 2
COLS = HEADS * HEAD
BLOCK = 384
PAIR = 2 * BLOCK
N_Y, N_Z = 4, 2
N_X, N_ZHI = 4, 4
HDR = 16
VMEM = pl.BlockSpec(memory_space=pltpu.VMEM)
HBM = pl.BlockSpec(memory_space=pltpu.HBM)


def call(body, outs, ins, scratch=(), flops=0, moved=0, hbm_at=(), limit=8 << 20):
    specs = [HBM if i in hbm_at else VMEM for i in range(len(ins))]
    single = not isinstance(outs, (list, tuple))
    return pl.pallas_call(
        body,
        out_shape=outs,
        in_specs=specs,
        out_specs=VMEM if single else [VMEM] * len(outs),
        scratch_shapes=list(scratch),
        compiler_params=pltpu.CompilerParams(vmem_limit_bytes=limit),
        cost_estimate=pl.CostEstimate(flops=flops, bytes_accessed=moved, transcendentals=0),
    )(*ins)


def head_place():
    place = lax.axis_index(HEAD_AXIS)
    return place // 4, (place // 2) % 2, place % 2


def seq_place():
    place = lax.axis_index(SEQ_AXIS)
    return place // 4, place % 4


def chip_index(shift):
    dy, dz = shift
    y, z, _ = head_place()
    return lax.rem(y + (dy + N_Y), N_Y) * N_Z + lax.rem(z + dz, N_Z)


def head_shift(value, dy=0, dz=0, core=0):
    pairs = []
    for i in range(16):
        y, z, c = i // 4, (i // 2) % 2, i % 2
        pairs.append((i, ((y + dy) % 4) * 4 + ((z + dz) % 2) * 2 + (c + core) % 2))
    return lax.ppermute(value, HEAD_AXIS, pairs)


def seq_shift(value, dx=0, dz=0):
    pairs = [(i, ((i // 4 + dz) % 4) * 4 + (i % 4 + dx) % 4) for i in range(16)]
    return lax.ppermute(value, SEQ_AXIS, pairs)


def load(weights, cotangent):
    def body(w_ref, g_ref, o_ref, og_ref, sem):
        copies = [pltpu.make_async_copy(g_ref, og_ref, sem.at[3])]
        copies += [pltpu.make_async_copy(w_ref.at[m], o_ref.at[m], sem.at[m]) for m in range(3)]
        for copy in copies:
            copy.start()
        for copy in copies:
            copy.wait()

    return call(
        body,
        [pltpu.VMEM(weights.shape, BF16), pltpu.VMEM(cotangent.shape, BF16)],
        [pltpu.with_memory_space_constraint(x, pltpu.HBM) for x in (weights, cotangent)],
        [pltpu.SemaphoreType.DMA((4,))],
        moved=2 * weights.size,
        hbm_at=(0, 1),
        limit=4 << 20,
    )


def project(shifts, blocks, weights, total):
    n = len(shifts)
    first = total is None

    def body(*refs):
        refs = list(refs)
        pairs = [tuple([refs.pop(0) for _ in part] for part in pair) for pair in blocks]
        w_ref = refs.pop(0)
        t_ref = None if first else refs.pop(0)
        o_ref, xcat = refs
        core = head_place()[2]
        for i, (own, other) in enumerate(pairs):
            for pieces, place in ((own, core), (other, 1 - core)):
                row = 0
                for piece in pieces:
                    height = piece.shape[0]
                    cols = pl.ds(pl.multiple_of(place * BLOCK, BLOCK), BLOCK)
                    xcat[i, row : row + height, cols] = piece[...]
                    row += height
        for i, shift in enumerate(shifts):
            rows = pl.ds(pl.multiple_of(chip_index(shift) * PAIR, PAIR), PAIR)
            for m in range(3):
                cols = slice(m * COLS, (m + 1) * COLS)
                part = jnp.dot(xcat[i], w_ref[m, rows, :], preferred_element_type=F32)
                if i == 0 and first:
                    o_ref[:, cols] = part
                elif i == 0:
                    o_ref[:, cols] = t_ref[:, cols] + part
                else:
                    o_ref[:, cols] += part

    return call(
        body,
        jax.ShapeDtypeStruct((ROWS, 3 * COLS), F32),
        [piece for pair in blocks for part in pair for piece in part] + [weights] + ([] if first else [total]),
        [pltpu.VMEM((n, ROWS, PAIR), BF16)],
        flops=2 * n * ROWS * PAIR * 3 * COLS,
        moved=n * 3 * PAIR * COLS * 2,
    )


def split(first, second):
    half = ROWS // 2

    def body(a_ref, b_ref, upper, lower):
        upper[...] = a_ref[:half, :]
        lower[...] = b_ref[half:, :]

    return call(
        body,
        [jax.ShapeDtypeStruct((half, BLOCK), BF16)] * 2,
        [first, second],
        moved=4 * half * BLOCK * 2,
    )


def project_halves(parts, weights, total):
    n = len(parts)

    def body(*refs):
        w_ref, t_ref, o_ref = refs[n:]
        place = head_place()[2]
        for m in range(3):
            cols = slice(m * COLS, (m + 1) * COLS)
            sums = t_ref[:, cols]
            for (shift, own_core, _), x_ref in zip(parts, refs):
                core = place if own_core else 1 - place
                block = chip_index(shift) * 2 + core
                rows = pl.ds(pl.multiple_of(block * BLOCK, BLOCK), BLOCK)
                sums = sums + jnp.dot(
                    x_ref[...], w_ref[m, rows, :], preferred_element_type=F32
                )
            o_ref[:, cols] = sums

    return call(
        body,
        jax.ShapeDtypeStruct((ROWS, 3 * COLS), F32),
        [block for _, _, block in parts] + [weights, total],
        flops=2 * n * ROWS * BLOCK * 3 * COLS,
        moved=n * 3 * BLOCK * COLS * 2,
    )


def running_sums(log_decay_row):
    def body(l_ref, c_ref, r_ref):
        i = lax.broadcasted_iota(jnp.int32, (ROWS, ROWS), 0)
        j = lax.broadcasted_iota(jnp.int32, (ROWS, ROWS), 1)
        lower = (i >= j).astype(F32)
        logs = jnp.concatenate([l_ref[...], jnp.zeros((8 - HEADS, ROWS), F32)], axis=0)
        nt = (((1,), (1,)), ((), ()))
        highest = lax.Precision.HIGHEST
        column = lax.dot_general(lower, logs, nt, precision=highest, preferred_element_type=F32)
        c_ref[...] = column[:, :HEADS]
        r_ref[...] = lax.dot_general(
            logs, lower, nt, precision=highest, preferred_element_type=F32
        )

    return call(
        body,
        [
            jax.ShapeDtypeStruct((ROWS, HEADS), F32),
            jax.ShapeDtypeStruct((8, ROWS), F32),
        ],
        [log_decay_row],
        flops=200 * ROWS * ROWS,
        moved=4 * HEADS * ROWS,
    )


def decay_matrix(running, running_row):
    def body(c_ref, r_ref, o_ref):
        i = lax.broadcasted_iota(jnp.int32, (ROWS, ROWS), 0)
        j = lax.broadcasted_iota(jnp.int32, (ROWS, ROWS), 1)
        causal = i >= j
        for h in range(HEADS):
            gap = c_ref[:, h : h + 1] - r_ref[h : h + 1, :]
            o_ref[h] = jnp.where(causal, jnp.exp(jnp.where(causal, gap, 0.0)), 0.0) * (
                HEAD**-0.5
            )

    return call(
        body,
        jax.ShapeDtypeStruct((HEADS, ROWS, ROWS), F32),
        [running, running_row],
        flops=10 * HEADS * ROWS * ROWS,
        moved=4 * HEADS * ROWS * ROWS,
    )


def local_states(projected, cotangent, running):
    def body(p_ref, g_ref, r_ref, q_ref, k_ref, v_ref, m_ref):
        last = r_ref[ROWS - 1 : ROWS, :]
        for h in range(HEADS):
            cols = slice(h * HEAD, (h + 1) * HEAD)
            query = jax.nn.silu(p_ref[:, cols]).astype(BF16)
            key = jax.nn.silu(p_ref[:, COLS + h * HEAD : COLS + (h + 1) * HEAD]).astype(BF16)
            value = p_ref[:, 2 * COLS + h * HEAD : 2 * COLS + (h + 1) * HEAD].astype(BF16)
            q_ref[:, cols], k_ref[:, cols], v_ref[:, cols] = query, key, value
            run = r_ref[:, h : h + 1]
            fall = jnp.exp(last[:, h : h + 1] - run)
            rise = jnp.exp(run)
            tn = (((0,), (0,)), ((), ()))
            key_state = lax.dot_general(
                (key.astype(F32) * fall).astype(BF16), value, tn, preferred_element_type=F32
            )
            query_state = lax.dot_general(
                (query.astype(F32) * rise).astype(BF16),
                g_ref[:, cols],
                tn,
                preferred_element_type=F32,
            )
            m_ref[h * HEAD : (h + 1) * HEAD, :] = key_state.astype(BF16)
            m_ref[COLS + h * HEAD : COLS + (h + 1) * HEAD, :] = query_state.astype(BF16)
        header(m_ref, 2 * COLS, [last[:, h : h + 1] for h in range(HEADS)])

    act = jax.ShapeDtypeStruct((ROWS, COLS), BF16)
    return call(
        body,
        [act, act, act, jax.ShapeDtypeStruct((2 * COLS + HDR, HEAD), BF16)],
        [projected, cotangent, running],
        flops=8 * ROWS * HEAD * COLS,
        moved=ROWS * COLS * 16,
    )


def header(ref, row, totals):
    sub = lax.broadcasted_iota(jnp.int32, (HDR, HEAD), 0)
    block = jnp.zeros((HDR, HEAD), F32)
    for h in range(HEADS):
        total = jnp.broadcast_to(totals[h], (HDR, HEAD))
        high = total.astype(BF16).astype(F32)
        block = jnp.where(sub == h, high, block)
        block = jnp.where(sub == HEADS + h, total - high, block)
    ref[row : row + HDR, :] = block.astype(BF16)


def read_totals(ref, row):
    block = ref[row : row + HDR, :].astype(F32)
    return [block[h : h + 1, :] + block[HEADS + h : HEADS + h + 1, :] for h in range(HEADS)]


def inner_part(query, key, value, cotangent, decays):
    def body(q_ref, k_ref, v_ref, g_ref, d_ref, gq_ref, gk_ref, gv_ref):
        nt = (((1,), (1,)), ((), ()))
        tn = (((0,), (0,)), ((), ()))
        for h in range(HEADS):
            cols = slice(h * HEAD, (h + 1) * HEAD)
            q, k, v, g = q_ref[:, cols], k_ref[:, cols], v_ref[:, cols], g_ref[:, cols]
            decay = d_ref[h]
            out_value = (
                lax.dot_general(g, v, nt, preferred_element_type=F32) * decay
            ).astype(BF16)
            query_key = (
                lax.dot_general(q, k, nt, preferred_element_type=F32) * decay
            ).astype(BF16)
            gq_ref[:, cols] = jnp.dot(out_value, k, preferred_element_type=F32)
            gk_ref[:, cols] = lax.dot_general(out_value, q, tn, preferred_element_type=F32)
            gv_ref[:, cols] = lax.dot_general(query_key, g, tn, preferred_element_type=F32)

    part = jax.ShapeDtypeStruct((ROWS, COLS), F32)
    return call(
        body,
        [part] * 3,
        [query, key, value, cotangent, decays],
        flops=10 * ROWS * ROWS * COLS,
        moved=ROWS * COLS * 20,
    )


def join_x(own, received):
    def body(own_ref, *refs):
        got = refs[:3]
        send = refs[3:6]
        keep_ref, scale_ref = refs[6:]
        z, x = seq_place()
        messages = [own_ref] + list(got)
        row = 2 * COLS
        totals = [read_totals(m, row) for m in messages]
        source = [lax.rem(x - s + N_X, N_X) for s in range(N_X)]
        for h in range(HEADS):
            zero = jnp.zeros((1, HEAD), F32)

            def between(low, high):
                out = zero
                for s in range(N_X):
                    inside = jnp.logical_and(source[s] > low, source[s] < high)
                    out = out + jnp.where(inside, totals[s][h], 0.0)
                return out

            key_all = jnp.zeros((HEAD, HEAD), F32)
            query_all = jnp.zeros((HEAD, HEAD), F32)
            key_before = jnp.zeros((HEAD, HEAD), F32)
            query_after = jnp.zeros((HEAD, HEAD), F32)
            for s in range(N_X):
                ks = messages[s][h * HEAD : (h + 1) * HEAD, :].astype(F32)
                qs = messages[s][COLS + h * HEAD : COLS + (h + 1) * HEAD, :].astype(F32)
                p = source[s]
                key_all += jnp.exp(between(p, N_X)) * ks
                query_all += jnp.exp(between(-1, p)) * qs
                if s:
                    key_before += jnp.where(p < x, jnp.exp(between(p, x)), 0.0) * ks
                    query_after += jnp.where(p > x, jnp.exp(between(x, p)), 0.0) * qs
            rows = slice(h * HEAD, (h + 1) * HEAD)
            keep_ref[rows, :] = key_before
            keep_ref[COLS + h * HEAD : COLS + (h + 1) * HEAD, :] = query_after
            scale_ref[h : h + 1, :] = jnp.exp(between(-1, x))
            scale_ref[HEADS + h : HEADS + h + 1, :] = jnp.exp(between(x, N_X))
            for s in range(1, N_ZHI):
                later = jnp.full((HEAD, HEAD), z + s) < N_ZHI
                send[s - 1][rows, :] = jnp.where(later, key_all, query_all).astype(BF16)
        group = [sum(totals[s][h] for s in range(N_X)) for h in range(HEADS)]
        for s in range(1, N_ZHI):
            header(send[s - 1], COLS, group)

    message = jax.ShapeDtypeStruct((COLS + HDR, HEAD), BF16)
    return call(
        body,
        [message] * 3
        + [jax.ShapeDtypeStruct((2 * COLS, HEAD), F32), jax.ShapeDtypeStruct((8, HEAD), F32)],
        [own] + list(received),
        flops=40 * COLS * HEAD,
        moved=COLS * HEAD * 20,
    )


def outer_part(received, keep, scale, projected, act, cotangent, inner, running):
    def body(*refs):
        got = refs[:3]
        keep_ref, scale_ref, p_ref, _, k_ref, v_ref, g_ref = refs[3:10]
        gq_ref, gk_ref, gv_ref, r_ref, o_ref = refs[10:]
        z, _ = seq_place()
        nt = (((1,), (1,)), ((), ()))
        source = [lax.rem(z - s + N_ZHI, N_ZHI) for s in range(1, N_ZHI)]
        totals = [read_totals(m, COLS) for m in got]
        c = HEAD**-0.5
        last = r_ref[ROWS - 1 : ROWS, :]

        def slope(v):
            s = jax.nn.sigmoid(v)
            return s * (1.0 + v * (1.0 - s))

        for h in range(HEADS):
            cols = slice(h * HEAD, (h + 1) * HEAD)

            def between(low, high):
                out = jnp.zeros((1, HEAD), F32)
                for s in range(N_ZHI - 1):
                    inside = jnp.logical_and(source[s] > low, source[s] < high)
                    out = out + jnp.where(inside, totals[s][h], 0.0)
                return out

            before = jnp.zeros((HEAD, HEAD), F32)
            after = jnp.zeros((HEAD, HEAD), F32)
            for s in range(N_ZHI - 1):
                p = source[s]
                state = got[s][cols, :].astype(F32)
                before += jnp.where(p < z, jnp.exp(between(p, z)), 0.0) * state
                after += jnp.where(p > z, jnp.exp(between(z, p)), 0.0) * state
            state_in = (keep_ref[cols, :] + scale_ref[h : h + 1, :] * before).astype(BF16)
            grad_in = (
                keep_ref[COLS + h * HEAD : COLS + (h + 1) * HEAD, :]
                + scale_ref[HEADS + h : HEADS + h + 1, :] * after
            ).astype(BF16)
            run = r_ref[:, h : h + 1]
            rise = jnp.exp(run) * c
            fall = jnp.exp(last[:, h : h + 1] - run) * c
            grad_query = gq_ref[:, cols] + rise * lax.dot_general(
                g_ref[:, cols], state_in, nt, preferred_element_type=F32
            )
            grad_key = gk_ref[:, cols] + fall * lax.dot_general(
                v_ref[:, cols], grad_in, nt, preferred_element_type=F32
            )
            grad_value = gv_ref[:, cols] + fall * jnp.dot(
                k_ref[:, cols], grad_in, preferred_element_type=F32
            )
            grads = (
                grad_query * slope(p_ref[:, cols]),
                grad_key * slope(p_ref[:, COLS + h * HEAD : COLS + (h + 1) * HEAD]),
                grad_value,
            )
            for m in range(3):
                at = m * COLS + h * HEAD
                o_ref[at : at + HEAD, :] = grads[m].T.astype(BF16)

    return call(
        body,
        jax.ShapeDtypeStruct((3 * COLS, ROWS), BF16),
        list(received) + [keep, scale, projected] + list(act) + [cotangent] + list(inner) + [running],
        flops=6 * ROWS * HEAD * COLS,
        moved=ROWS * COLS * 40,
    )


def partials(shifts, grads, weights, received, own_core, dtype=BF16):
    n = len(shifts)
    add = received is not None

    def body(*refs):
        refs = list(refs)
        g_ref, w_ref = refs.pop(0), refs.pop(0)
        r_ref = refs.pop(0) if add else None
        outs = refs
        core = head_place()[2]
        if not own_core:
            core = 1 - core
        for i, shift in enumerate(shifts):
            block = chip_index(shift) * 2 + core
            rows = pl.ds(pl.multiple_of(block * BLOCK, BLOCK), BLOCK)
            part = None
            for m in range(3):
                term = jnp.dot(
                    w_ref[m, rows, :],
                    g_ref[m * COLS : (m + 1) * COLS, :],
                    preferred_element_type=F32,
                )
                part = term if part is None else part + term
            if add:
                outs[i][...] = (part + r_ref[i].astype(F32)).astype(BF16)
            else:
                outs[0][i] = part.astype(dtype)

    block = jax.ShapeDtypeStruct((BLOCK, ROWS), BF16)
    return call(
        body,
        [block] * n if add else [jax.ShapeDtypeStruct((n, BLOCK, ROWS), dtype)],
        [grads, weights] + ([received] if add else []),
        flops=2 * n * ROWS * BLOCK * 3 * COLS,
        moved=n * 3 * BLOCK * COLS * 2,
    )


def add_cores(own, received):
    def body(a_ref, b_ref, *outs):
        for i, out in enumerate(outs):
            out[...] = (a_ref[i] + b_ref[i].astype(F32)).astype(BF16)

    n = own.shape[0]
    return call(
        body,
        [jax.ShapeDtypeStruct((BLOCK, ROWS), BF16)] * n,
        [own, received],
        flops=n * BLOCK * ROWS,
        moved=n * BLOCK * ROWS * 8,
    )


def add_all(parts):
    def body(*refs):
        total = refs[0][...].astype(F32)
        for ref in refs[1:-1]:
            total = total + ref[...].astype(F32)
        refs[-1][...] = total.astype(BF16)

    return call(
        body,
        jax.ShapeDtypeStruct((BLOCK, ROWS), BF16),
        list(parts),
        flops=len(parts) * BLOCK * ROWS,
        moved=BLOCK * ROWS * 2 * (len(parts) + 1),
    )


def finish(parts):
    def body(*refs):
        total = refs[0][...].astype(F32)
        for ref in refs[1:-1]:
            total = total + ref[...].astype(F32)
        refs[-1][...] = total.T.astype(BF16)

    return call(
        body,
        jax.ShapeDtypeStruct((ROWS, BLOCK), BF16),
        list(parts),
        flops=5 * BLOCK * ROWS,
        moved=BLOCK * ROWS * 12,
    )


OWN, FAR, UP, DOWN = (0, 0), (2, 0), (-1, 0), (1, 0)
SIDE, FAR_SIDE, UP_SIDE, DOWN_SIDE = (0, 1), (2, 1), (-1, 1), (1, 1)
GROUPS = (
    ((DOWN_SIDE,), True),
    ((FAR_SIDE,), True),
    ((UP_SIDE, FAR), True),
    ((DOWN, UP), False),
    ((SIDE, OWN), False),
)


def layer(inputs, weights, cotangent, log_decay):
    running, running_row = running_sums(log_decay.T)
    decays = decay_matrix(running, running_row)

    side = head_shift(inputs, dz=1)
    up = head_shift(inputs, dy=1)
    down = head_shift(inputs, dy=-1)
    upper, lower = split(up, down)
    upper = head_shift(upper, dy=1)
    lower = head_shift(lower, dy=-1)
    up_side = head_shift(up, dz=1)
    far_side = head_shift(side, dy=2)
    down_side = head_shift(down, dz=1)

    def both(block):
        return ([block], [head_shift(block, core=1)])

    resident, cotangent = load(weights, cotangent)
    total = project([OWN], [both(inputs)], resident, None)
    total = project([UP, SIDE, DOWN], [both(up), both(side), both(down)], resident, total)
    total = project([UP_SIDE], [both(up_side)], resident, total)
    (_, [upper_other]), (_, [lower_other]) = both(upper), both(lower)
    total = project([FAR], [([upper, lower], [upper_other, lower_other])], resident, total)
    _, [far_other] = both(far_side)
    _, [down_other] = both(down_side)
    total = project_halves([(FAR_SIDE, True, far_side)], resident, total)
    total = project_halves(
        [(FAR_SIDE, False, far_other), (DOWN_SIDE, True, down_side)], resident, total
    )
    total = project_halves([(DOWN_SIDE, False, down_other)], resident, total)

    query, key, value, message = local_states(total, cotangent, running)
    over_x = [seq_shift(message, dx=s) for s in (1, 2, 3)]
    inner = inner_part(query, key, value, cotangent, decays)
    *send, keep, scale = join_x(message, over_x)
    over_z = [seq_shift(send[s - 1], dz=s) for s in (1, 2, 3)]
    grads = outer_part(
        over_z, keep, scale, total, (query, key, value), cotangent, inner, running
    )

    blocks = {}
    for group, apart in GROUPS:
        (share,) = partials(group, grads, resident, None, False)
        got = head_shift(share, core=1)
        if apart:
            (own,) = partials(group, grads, resident, None, True, F32)
            done = add_cores(own, got)
        else:
            done = partials(group, grads, resident, got, True)
        blocks.update(zip(group, done))
    down_side = head_shift(blocks[DOWN_SIDE], dz=1)
    far_side = head_shift(blocks[FAR_SIDE], dy=2)
    up_side = head_shift(blocks[UP_SIDE], dz=1)
    far = head_shift(blocks[FAR], dy=2)
    down = head_shift(add_all([blocks[DOWN], down_side]), dy=1)
    side = head_shift(add_all([blocks[SIDE], far_side]), dz=1)
    up = head_shift(add_all([blocks[UP], up_side]), dy=-1)
    return finish([blocks[OWN], far, down, up, side])


def solution(mesh):
    rows = P(SEQ_AXIS, HEAD_AXIS)
    return jax.shard_map(
        layer,
        mesh=mesh,
        in_specs=(rows, P(None, None, HEAD_AXIS), rows, rows),
        out_specs=rows,
        check_vma=False,
    )
```
